32 devices in a mesh: curve: 4 (over x, core), seg: 8 (over z, y).
Axes of the slice: x: 2, y: 2, z: 4, core: 2. Of those that a mesh axis runs over, the one named last changes fastest.
Arguments:
- adjoint: float32 [9, 2048, 512], P(None, ('curve', 'seg')), may hold values from -6 to 6
- material: float32 [3, 2048], P(None, ('curve', 'seg')), may hold values from 0.5 to 2
- face_partner: int32 [2048, 6], P(('curve', 'seg')), may hold values from 0 to 447, as said below
- send_faces: int32 [32, 4, 16], P(('curve', 'seg')), may hold values from 0 to 383, as said below
- migration: int32 [3, 2048], P(None, ('curve', 'seg')), may hold values from 0 to 7, as said below
- children: int32 [2, 256], P(None, ('curve', 'seg')), may hold values from -1 to 7, as said below
Outputs:
- adjoint_next: float32 [9, 2048, 512], P(None, ('curve', 'seg'))
- parent_adjoint: float32 [9, 256, 512], P(None, ('curve', 'seg'))
The draws below stay inside these ranges and needn't reach their ends.
Inputs may be any that keep to these rules, and one draw needn't show every extreme that they name: `face_partner`: entries below 384 name a face of the same partition; the others name a slot of a side's received faces as in the reference program. Each face is the partner of exactly one face. `send_faces`: slot t of side -x or +x is the face at position (t // 4, t % 4) in (y, z), of side -y or +y at (x, z); entries are 6 l + f of this partition's elements. `migration`: the eight children of each parent lie on one partition of the owner's segment group, one per octant. Each partition keeps all children of 4 of its own parents (row 1 is then the parent) and holds the children of 4 foreign parents (row 1 is then the slot, below 2, unique per owner). At most 2 foreign parents of one owner lie on one partition, and some partition holds exactly 2 for some owner. Row 0 is the owner itself with row 1 equal to -1 for the 4 parents whose children stayed; otherwise the holder and the slot of the matching migration entry.
All inputs are finite; a program needn't handle non-finite values.
Results may differ from the reference program's by a relative error of at most 0.000052.
Values sent between devices are 32-bit elements; how exact they have to be, the bound alone decides.
A program may use at most 128 MiB of HBM per device.

```python
import math
import jax
import jax.numpy as jnp
import numpy as np
from jax import lax

NP = 8
NODES = 512
FACE = 64
BXY = 4
BZ = 4
E_DEV = 64
CAP = 16
P_DEV = 8
MIG_CAP = 2
ELEMENTS = 2048
PARENTS = 256
N_CURVE = 4
N_SEG = 8


def brick_orders(key):
    devices = ELEMENTS // E_DEV
    base_key = jax.random.fold_in(key, 11)

    def device_order(device):
        return jax.random.permutation(jax.random.fold_in(base_key, device), E_DEV).astype(jnp.int32)
    return jax.vmap(device_order)(jnp.arange(devices))


def cell_number(along_x, along_y, along_z):
    return (along_x * BXY + along_y) * BZ + along_z


def device_faces(cell_order):
    cell_ids = jnp.arange(E_DEV)
    along_x = cell_ids // (BXY * BZ)
    along_y = cell_ids // BZ % BXY
    along_z = cell_ids % BZ
    remote = 6 * E_DEV
    across_x = along_y * BZ + along_z
    across_y = along_x * BZ + along_z
    lower_x = jnp.where(along_x > 0, cell_order[cell_number(jnp.maximum(along_x - 1, 0), along_y, along_z)] * 6 + 1, remote + across_x)
    upper_x = jnp.where(along_x < BXY - 1, cell_order[cell_number(jnp.minimum(along_x + 1, BXY - 1), along_y, along_z)] * 6 + 0, remote + CAP + across_x)
    lower_y = jnp.where(along_y > 0, cell_order[cell_number(along_x, jnp.maximum(along_y - 1, 0), along_z)] * 6 + 3, remote + 2 * CAP + across_y)
    upper_y = jnp.where(along_y < BXY - 1, cell_order[cell_number(along_x, jnp.minimum(along_y + 1, BXY - 1), along_z)] * 6 + 2, remote + 3 * CAP + across_y)
    lower_z = cell_order[cell_number(along_x, along_y, (along_z - 1) % BZ)] * 6 + 5
    upper_z = cell_order[cell_number(along_x, along_y, (along_z + 1) % BZ)] * 6 + 4
    by_cell = jnp.stack([lower_x, upper_x, lower_y, upper_y, lower_z, upper_z], axis=1).astype(jnp.int32)
    partner = jnp.zeros((E_DEV, 6), jnp.int32).at[cell_order].set(by_cell)
    slot_ids = jnp.arange(CAP)
    outer_pos = slot_ids // BZ
    inner_pos = slot_ids % BZ
    send_lists = jnp.stack([cell_order[cell_number(0, outer_pos, inner_pos)] * 6 + 0, cell_order[cell_number(BXY - 1, outer_pos, inner_pos)] * 6 + 1, cell_order[cell_number(outer_pos, 0, inner_pos)] * 6 + 2, cell_order[cell_number(outer_pos, BXY - 1, inner_pos)] * 6 + 3]).astype(jnp.int32)
    return (partner, send_lists)


def draw_face_partner(key, part):
    partner, send_lists = jax.vmap(device_faces)(brick_orders(key))
    return partner.reshape(ELEMENTS, 6).astype(jnp.int32)


def draw_send_faces(key, part):
    partner, send_lists = jax.vmap(device_faces)(brick_orders(key))
    return send_lists.astype(jnp.int32)


def migration_tables(key):
    base_key = jax.random.fold_in(key, 23)
    half_count = P_DEV // 2

    def group_tables(group):
        group_keys = jax.random.split(jax.random.fold_in(base_key, group), 4)
        arrangement = jax.random.permutation(group_keys[0], N_SEG).astype(jnp.int32)
        full_offset = jax.random.randint(group_keys[1], (), 0, N_SEG - 1)
        weights = jnp.zeros((N_SEG - 1,), jnp.int32).at[full_offset].set(MIG_CAP)
        random_picks = jax.random.randint(group_keys[2], (half_count - MIG_CAP,), 0, N_SEG - 1)
        offsets = jnp.arange(N_SEG - 1)

        def assign_unit(current, pick_value):
            distance = (offsets - pick_value) % (N_SEG - 1)
            priority = jnp.where(current < MIG_CAP, distance, 4 * N_SEG)
            return (current.at[jnp.argmin(priority)].add(1), None)
        weights, unused = lax.scan(assign_unit, weights, random_picks)
        upper_sum = jnp.cumsum(weights)
        lower_sum = upper_sum - weights
        moving = jnp.arange(half_count)
        offset_rank = jnp.sum(moving[:, None] >= upper_sum[None, :], axis=1)
        slot_index = (moving - lower_sum[offset_rank]).astype(jnp.int32)
        offset_step = offset_rank + 1

        def member(position):
            member_keys = jax.random.split(jax.random.fold_in(group_keys[3], position), 2)
            element_order = jax.random.permutation(member_keys[0], E_DEV)
            parent_order = jax.random.permutation(member_keys[1], P_DEV).astype(jnp.int32)
            holder = arrangement[position]
            owners = arrangement[(position + offset_step) % N_SEG]
            sources = arrangement[(position - offset_step) % N_SEG]
            group_owner = jnp.concatenate([jnp.full((half_count,), holder, jnp.int32), owners])
            group_slot = jnp.concatenate([parent_order[:half_count], slot_index])
            local_ids = jnp.arange(E_DEV)
            values = jnp.stack([group_owner[local_ids // 8], group_slot[local_ids // 8], (local_ids % 8).astype(jnp.int32)])
            moved = jnp.zeros((3, E_DEV), jnp.int32).at[:, element_order].set(values)
            parent_values = jnp.stack([jnp.concatenate([jnp.full((half_count,), holder, jnp.int32), sources]), jnp.concatenate([jnp.full((half_count,), -1, jnp.int32), slot_index])])
            owned = jnp.zeros((2, P_DEV), jnp.int32).at[:, parent_order].set(parent_values)
            return (moved, owned)
        moved, owned = jax.vmap(member)(jnp.arange(N_SEG))
        inverse = jnp.argsort(arrangement)
        return (moved[inverse], owned[inverse])
    moved, owned = jax.vmap(group_tables)(jnp.arange(N_CURVE))
    moved = jnp.transpose(moved, (2, 0, 1, 3)).reshape(3, ELEMENTS)
    owned = jnp.transpose(owned, (2, 0, 1, 3)).reshape(2, PARENTS)
    return (moved.astype(jnp.int32), owned.astype(jnp.int32))


def draw_migration(key, part):
    moved, owned = migration_tables(key)
    return moved


def draw_children(key, part):
    moved, owned = migration_tables(key)
    return owned


def block_levels(key, dims, shards, low, largest):
    factor_of = 1.0
    for axis_at, blocks in shards:
        heights = jax.random.uniform(jax.random.fold_in(jax.random.fold_in(key, 6), axis_at), (blocks,), jnp.float32, low / len(shards), largest / len(shards))
        factor_of = factor_of * jnp.repeat(jnp.exp(heights), dims[axis_at] // blocks).reshape((-1,) + (1,) * (len(dims) - 1 - axis_at))
    return factor_of


def bell_draw(rng, dims, deviation, most, pieces=(), kind=jnp.bfloat16):
    level = block_levels(rng, dims, pieces, -0.22, 0.18) if pieces else 1.0
    values = jax.random.normal(rng, dims, jnp.float32) * deviation * level
    return jnp.minimum(jnp.maximum(values, -most), most).astype(kind)


def setup_inputs(seed: int = 0) -> dict:
    keys = jax.random.split(jax.random.key(seed), 7)
    adjoint = bell_draw(keys[0], (9, ELEMENTS, NODES), 1.0, 6.0, ((1, 32),), jnp.float32)
    material = jnp.clip(jnp.exp(math.log(2.0) - 1.3862944 * jax.random.uniform(keys[1], (3, ELEMENTS), jnp.float32) ** block_levels(keys[1], (3, ELEMENTS), ((1, 32),), -0.2, 0.2)), 0.5, 2.0)
    face_partner = draw_face_partner(jax.random.fold_in(keys[6], 71), 0)
    send_faces = draw_send_faces(jax.random.fold_in(keys[6], 71), 0)
    migration = draw_migration(jax.random.fold_in(keys[6], 71), 0)
    children = draw_children(jax.random.fold_in(keys[6], 71), 0)
    return {"adjoint": adjoint, "material": material, "face_partner": face_partner, "send_faces": send_faces, "migration": migration, "children": children}


voigt_index = ((3, 8, 7), (8, 4, 6), (7, 6, 5))
courant = 0.8


def lobatto_nodes(edge_nodes):
    return -np.cos(np.pi * np.arange(edge_nodes) / (edge_nodes - 1))


def derivative_line(edge_nodes):
    points = lobatto_nodes(edge_nodes)
    node_ids = np.arange(edge_nodes)
    weight = np.where((node_ids == 0) | (node_ids == edge_nodes - 1), 2.0, 1.0)
    row_ids = node_ids[:, None]
    column_ids = node_ids[None, :]
    differ = points[:, None] - points[None, :]
    safe_gap = np.where(row_ids == column_ids, 1.0, differ)
    matrix = (weight[:, None] / weight[None, :]) * (-1.0) ** (row_ids + column_ids) / safe_gap
    matrix = np.where(row_ids == column_ids, 0.0, matrix)
    return matrix - np.eye(edge_nodes) * matrix.sum(axis=1)[:, None]


def derivative_stack(edge_nodes):
    line_matrix = derivative_line(edge_nodes)
    identity = np.eye(edge_nodes)
    blocks = [np.kron(np.kron(line_matrix, identity), identity), np.kron(np.kron(identity, line_matrix), identity), np.kron(np.kron(identity, identity), line_matrix)]
    return jnp.asarray(np.concatenate(blocks, axis=0), dtype=jnp.float32)


def refine_line(edge_nodes, upper):
    points = lobatto_nodes(edge_nodes)
    targets = (points + (2.0 * upper - 1.0)) / 2.0
    columns = []
    for column in range(edge_nodes):
        factor = np.ones(edge_nodes)
        for other_node in range(edge_nodes):
            if other_node != column:
                factor = factor * (targets - points[other_node]) / (points[column] - points[other_node])
        columns.append(factor)
    return np.stack(columns, axis=1)


def refine_stack(edge_nodes):
    blocks = []
    for octant in range(8):
        blocks.append(np.kron(np.kron(refine_line(edge_nodes, (octant // 4) % 2), refine_line(edge_nodes, (octant // 2) % 2)), refine_line(edge_nodes, octant % 2)))
    return jnp.asarray(np.concatenate(blocks, axis=0), dtype=jnp.float32)


def material_image(field_state, inv_density, lame_first, shear_modulus, direction):
    trace_sum = field_state[3] + field_state[4] + field_state[5]
    velocity = []
    for component in range(3):
        velocity_term = shear_modulus * field_state[voigt_index[direction][component]]
        if component == direction:
            velocity_term = 2.0 * velocity_term + lame_first * trace_sum
        velocity.append(velocity_term)
    stress = [inv_density * field_state[component] for component in range(3)]
    return jnp.stack(velocity), jnp.stack(stress)


def place_rows(velocity, stress, direction):
    zero_row = jnp.zeros_like(velocity[0])
    row_list = [velocity[0], velocity[1], velocity[2]] + [zero_row] * 6
    for component in range(3):
        row_list[voigt_index[component][direction]] = stress[component]
    return jnp.stack(row_list)


def face_selector(face_id, edge_nodes):
    plane_index = 0 if face_id % 2 == 0 else edge_nodes - 1
    selector = [slice(None)] * 5
    selector[2 + face_id // 2] = plane_index
    return tuple(selector)


def volume_term(field_state, materials, derivative):
    elements = field_state.shape[1]
    columns = []
    for direction in range(3):
        velocity, stress = material_image(field_state, materials[0][:, None], materials[1][:, None], materials[2][:, None], direction)
        columns.append(place_rows(velocity, stress, direction))
    stacked = jnp.concatenate(columns, axis=2).reshape(9 * elements, 3 * field_state.shape[2])
    product = jnp.dot(stacked, derivative, precision=lax.Precision.HIGHEST, preferred_element_type=jnp.float32)
    return product.reshape(9, elements, field_state.shape[2])


def image_of_faces(traces, inv_density, lame_first, shear_modulus):
    parts = []
    for direction in range(3):
        face_part = traces[:, :, 2 * direction:2 * direction + 2]
        velocity, stress = material_image(face_part, inv_density[:, None, None], lame_first[:, None, None], shear_modulus[:, None, None], direction)
        parts.append(jnp.concatenate([velocity, stress], axis=0))
    return jnp.concatenate(parts, axis=2)


def add_faces(result, face_total, edge_nodes):
    elements = face_total.shape[1]
    lift = 0.5 * edge_nodes * (edge_nodes - 1)
    for face_id in range(6):
        lift_factor = 0.5 * lift if face_id % 2 == 0 else -0.5 * lift
        piece = lift_factor * face_total[:, :, face_id]
        row_block = place_rows(piece[0:3], piece[3:6], face_id // 2)
        result = result.at[face_selector(face_id, edge_nodes)].add(row_block.reshape(9, elements, edge_nodes, edge_nodes))
    return result


def runge_step(field_state, operator, time_step):
    section_one = operator(field_state)
    section_two = operator(field_state + 0.5 * time_step * section_one)
    section_three = operator(field_state + 0.5 * time_step * section_two)
    section_four = operator(field_state + time_step * section_three)
    return field_state + (time_step / 6.0) * (section_one + 2.0 * section_two + 2.0 * section_three + section_four)


def reference(adjoint, material, face_partner, send_faces, migration, children):
    elements = adjoint.shape[1]
    devices = elements // E_DEV
    derivative = derivative_stack(NP)
    inv_density = 1.0 / material[0]
    lame_first = material[1]
    shear_modulus = material[2]
    materials = jnp.moveaxis(jnp.stack([inv_density, lame_first, shear_modulus]).reshape(3, devices, E_DEV), 1, 0)

    def block_volume(block_pair):
        return volume_term(block_pair[0], block_pair[1], derivative)

    def operator(field_state):
        blocks = jnp.moveaxis(field_state.reshape(9, devices, E_DEV, NODES), 1, 0)
        volume = lax.map(block_volume, (blocks, materials))
        result = jnp.moveaxis(volume, 0, 1).reshape(9, elements, NP, NP, NP)
        node_cube = field_state.reshape(9, elements, NP, NP, NP)
        traces = jnp.stack([node_cube[face_selector(face_id, NP)].reshape(9, elements, FACE) for face_id in range(6)], axis=2)
        face_image = image_of_faces(traces, inv_density, lame_first, shear_modulus)
        local_table = face_image.reshape(6, devices, E_DEV * 6, FACE)
        sent_rows = jnp.take_along_axis(local_table, send_faces.reshape(1, devices, 4 * CAP, 1), axis=2).reshape(6, N_CURVE, N_SEG, 4, CAP, FACE)
        received = jnp.stack([jnp.roll(sent_rows[:, :, :, 1], 1, axis=1), jnp.roll(sent_rows[:, :, :, 0], -1, axis=1), jnp.roll(sent_rows[:, :, :, 3], 1, axis=2), jnp.roll(sent_rows[:, :, :, 2], -1, axis=2)], axis=3).reshape(6, devices, 4 * CAP, FACE)
        image_table = jnp.concatenate([local_table, received], axis=2)
        partner_image = jnp.take_along_axis(image_table, face_partner.reshape(1, devices, E_DEV * 6, 1), axis=2).reshape(6, elements, 6, FACE)
        return add_faces(result, face_image + partner_image, NP).reshape(9, elements, NODES)

    adjoint_next = runge_step(adjoint, operator, courant / (NP * NP))

    element_ids = jnp.arange(elements, dtype=jnp.int32)
    device_ids = element_ids // E_DEV
    own_seg = device_ids % N_SEG
    owner_device = (device_ids // N_SEG) * N_SEG + migration[0]
    parent_ids = jnp.arange(PARENTS, dtype=jnp.int32)
    parent_device = parent_ids // P_DEV
    migrated = children[1] >= 0
    table_size = devices * N_SEG * MIG_CAP
    lookup_key = jnp.where(migrated, (parent_device * N_SEG + children[0]) * MIG_CAP + jnp.maximum(children[1], 0), table_size).astype(jnp.int32)
    lookup = jnp.zeros((table_size,), jnp.int32).at[lookup_key].set((parent_ids % P_DEV).astype(jnp.int32), mode="drop")
    stays_home = migration[0] == own_seg
    remote_key = ((owner_device * N_SEG + own_seg) * MIG_CAP + jnp.clip(migration[1], 0, MIG_CAP - 1)).astype(jnp.int32)
    local_parent = jnp.where(stays_home, migration[1], lookup[remote_key])
    position = ((owner_device * P_DEV + local_parent) * 8 + migration[2]).astype(jnp.int32)
    placed = jnp.zeros((9, PARENTS * 8, NODES), jnp.float32).at[:, position].set(adjoint_next)
    parent_adjoint = jnp.dot(placed.reshape(9 * PARENTS, 8 * NODES), refine_stack(NP), precision=lax.Precision.HIGHEST, preferred_element_type=jnp.float32).reshape(9, PARENTS, NODES)
    return adjoint_next, parent_adjoint
```

```python
import functools

import jax
import jax.numpy as jnp
import numpy as np
from jax import lax
from jax.experimental import pallas as pl
from jax.experimental.pallas import tpu as pltpu
from jax.sharding import PartitionSpec as P

V = ((3, 8, 7), (8, 4, 6), (7, 6, 5))
F32 = jnp.float32
BF16 = jnp.bfloat16
NP = 8
NODES = NP**3
FACE = NP**2
HALF = NODES // 2
STEP = 0.8 / NP**2
GAIN = 0.5 * 0.5 * NP * (NP - 1)
SLOTS = 2


def lobatto_nodes():
    return -np.cos(np.pi * np.arange(NP) / (NP - 1))


def derivative_line():
    points = lobatto_nodes()
    ids = np.arange(NP)
    weight = np.where((ids == 0) | (ids == NP - 1), 2.0, 1.0)
    row, col = ids[:, None], ids[None, :]
    gap = np.where(row == col, 1.0, points[:, None] - points[None, :])
    matrix = weight[:, None] / weight[None, :] * (-1.0) ** (row + col) / gap
    matrix = np.where(row == col, 0.0, matrix)
    return matrix - np.eye(NP) * matrix.sum(axis=1)[:, None]


def refine_line(upper):
    points = lobatto_nodes()
    targets = (points + (2.0 * upper - 1.0)) / 2.0
    columns = []
    for column in range(NP):
        factor = np.ones(NP)
        for other in range(NP):
            if other != column:
                factor = factor * (targets - points[other]) / (points[column] - points[other])
        columns.append(factor)
    return np.stack(columns, axis=1)


def two_parts(matrix):
    matrix = np.asarray(matrix, np.float32)
    high = matrix.astype(jnp.bfloat16)
    low = (matrix - high.astype(np.float32)).astype(jnp.bfloat16)
    return high, low


def three_deep(matrix):
    high, low = two_parts(matrix)
    return np.concatenate([high, high, low], axis=0)


def line_operators(line):
    return (
        np.kron(line, np.eye(FACE)),
        np.kron(np.kron(np.eye(4), line), np.eye(NP)),
        np.kron(np.eye(32), line),
    )


def constants():
    line = derivative_line()
    line[0, 0] += GAIN
    line[NP - 1, NP - 1] -= GAIN
    derivs = [three_deep(m) for m in line_operators(line)]
    ids = np.arange(NODES).reshape(NP, NP, NP)
    selects, spreads = [], []
    for d in (1, 2):
        select = np.zeros((2, NODES, 2, 2, FACE))
        spread = np.zeros((2, FACE, NODES))
        for s in range(2):
            nodes = np.take(ids, 0 if s == 0 else NP - 1, axis=d).reshape(-1)
            spread[s, np.arange(FACE), nodes] = GAIN if s == 0 else -GAIN
            for h in range(2):
                select[h, nodes, s, h, np.arange(FACE)] = 1.0
        selects.append(select.reshape(2 * NODES, 4 * FACE).astype(jnp.bfloat16))
        spread = spread.reshape(2 * FACE, NODES).astype(jnp.bfloat16)
        spreads.append(np.concatenate([spread, spread], axis=0))
    lower = line_operators(refine_line(0))
    upper = line_operators(refine_line(1))
    refines = [three_deep(np.concatenate([a, b], axis=0)) for a, b in zip(lower, upper)]
    return derivs + selects + spreads + refines


def split(x):
    high = x.astype(BF16)
    return high, (x - high.astype(F32)).astype(BF16)


def dot(a, b):
    return jnp.dot(a, b, preferred_element_type=F32)


def iota(shape, dim):
    return lax.broadcasted_iota(jnp.int32, shape, dim)


def column(row, count):
    n = row.shape[1]
    hit = iota((count, n), 0) % n == iota((count, n), 1)
    return jnp.sum(jnp.where(hit, jnp.broadcast_to(row, (count, n)), 0.0), axis=1, keepdims=True)


def kernel(
    n_curve, n_seg, e, cap, parents,
    mat, partner, send, mig, child, *refs
):
    hbm, refs = refs[:11], refs[11:]
    (
        out, par,
        adj, d0, d1, d2, e1, e2, s1, s2, r0, r1, r2,
        w, xh, xl, vol, table, far_table, pick, far_pick, sendpick,
        outbox, inbox, pay, arrived,
        load_sem, send_sem, recv_sem, mig_send, mig_recv,
    ) = refs
    homes = (adj, d0, d1, d2, e1, e2, s1, s2, r0, r1, r2)
    loads = [
        pltpu.make_async_copy(hbm[k], homes[k], load_sem.at[k]) for k in range(len(homes))
    ]
    loads.append(pltpu.make_async_copy(hbm[0], out, load_sem.at[11]))
    loads.append(pltpu.make_async_copy(hbm[0], w, load_sem.at[12]))
    early = (12, 0, 4, 5, 1, 2, 3, 11, 6, 7)
    ci = lax.axis_index("curve")
    si = lax.axis_index("seg")
    cm = lax.rem(ci + n_curve - 1, n_curve)
    cp = lax.rem(ci + 1, n_curve)
    sm = lax.rem(si + n_seg - 1, n_seg)
    sp = lax.rem(si + 1, n_seg)
    sides = ((cm, si), (cp, si), (ci, sm), (ci, sp))
    barrier = pltpu.get_barrier_semaphore()
    MESH = pl.DeviceIdType.MESH
    for c in (cm, cp):
        pl.semaphore_signal(barrier, inc=1, device_id=(c, si), device_id_type=MESH)
    for k in range(1, n_seg):
        pl.semaphore_signal(
            barrier, inc=1, device_id=(ci, lax.rem(si + k, n_seg)), device_id_type=MESH
        )

    for k in early + (10, 9, 8):
        loads[k].start()

    faces = 6 * e
    pair = 2 * cap
    derivs = (d0, d1, d2)

    def codes(rows):
        k = iota((rows, faces), 1)
        return (6 * (k % e) + k // e).astype(F32)

    code = codes(e)
    for f in range(6):
        want = column(partner[f : f + 1, :].astype(F32), e)
        hit = jnp.where(code == want, 1.0, 0.0).astype(BF16)
        pick[f * e : (f + 1) * e, :] = jnp.concatenate([hit, hit], axis=1)
        if f < 4:
            slot_code = (iota((e, pair), 1) + faces + (f // 2) * pair).astype(F32)
            far = jnp.where(slot_code == want, 1.0, 0.0).astype(BF16)
            far_pick[f * e : (f + 1) * e, :] = jnp.concatenate([far, far], axis=1)
    for r in range(4):
        k = iota((cap, 2 * e), 1)
        code = (6 * (k % e) + k // e + 2 * (r // 2)).astype(F32)
        want = column(send[0, r : r + 1, :].astype(F32), cap)
        hit = jnp.where(code == want, 1.0, 0.0).astype(BF16)
        sendpick[r * cap : (r + 1) * cap, :] = jnp.concatenate([hit, hit], axis=1)

    density = jnp.broadcast_to(1.0 / column(mat[0:1, :], e), (e, NODES))
    lame = jnp.broadcast_to(column(mat[1:2, :], e), (e, NODES))
    shear = jnp.broadcast_to(column(mat[2:3, :], e), (e, NODES))

    vol[...] = jnp.zeros_like(vol)
    for k in early[:1] + early[2:3]:
        loads[k].wait()
    low_half = iota((e, 2 * FACE), 1) < FACE

    def comps(d):
        return [V[d][0] - 3, V[d][1] - 3, V[d][2] - 3, 6, 7, 8]

    def rows(d):
        return [0, 1, 2, V[0][d], V[1][d], V[2][d]]

    def share(step):
        return jnp.where((step == 0) | (step == 3), STEP / 6.0, STEP / 3.0).astype(F32)

    def put_trace(d, sel):
        cd = comps(d)
        blocks = []
        for src in (xh, xl):
            for p in range(3):
                a, b = cd[2 * p], cd[2 * p + 1]
                blocks.append(
                    jnp.concatenate(
                        [src[a * e : (a + 1) * e, :], src[b * e : (b + 1) * e, :]], axis=1
                    )
                )
        got = dot(jnp.concatenate(blocks, axis=0), sel[...]).astype(BF16)
        for part in range(2):
            for p in range(3):
                for s in range(2):
                    top = part * faces + (2 * d + s) * e
                    table[top : top + e, p * 2 * FACE : (p + 1) * 2 * FACE] = got[
                        (part * 3 + p) * e : (part * 3 + p + 1) * e,
                        s * 2 * FACE : (s + 1) * 2 * FACE,
                    ]

    def send_side(step, d):
        top = 2 * d * e
        source = jnp.concatenate(
            [table[top : top + 2 * e, :], table[faces + top : faces + top + 2 * e, :]], axis=0
        )
        picked = dot(sendpick[d * pair : (d + 1) * pair, :], source)
        outbox[step, 2 * d : 2 * d + 2] = picked.reshape(2, cap, 6 * FACE)
        copies = []
        for r in (2 * d, 2 * d + 1):
            copy = pltpu.make_async_remote_copy(
                src_ref=outbox.at[step, r],
                dst_ref=inbox.at[step, r ^ 1],
                send_sem=send_sem.at[step, r],
                recv_sem=recv_sem.at[step, r ^ 1],
                device_id=sides[r],
                device_id_type=MESH,
            )
            copy.start()
            copies.append(copy)
        return copies

    def onto_first(first, last):
        first, last = first * GAIN, last * -GAIN
        pieces = []
        for c in range(6):
            p, odd = c // 2, c % 2
            a = first[:, p * 2 * FACE : (p + 1) * 2 * FACE]
            b = last[:, p * 2 * FACE : (p + 1) * 2 * FACE]
            if odd:
                a = pltpu.roll(a, FACE, 1)
            else:
                b = pltpu.roll(b, FACE, 1)
            pieces.append((jnp.where(low_half, a, 0.0), jnp.where(low_half, 0.0, b)))
        return pieces

    def face_rows(lower, upper):
        blocks = []
        for c in range(6):
            p, odd = c // 2, c % 2
            a = lower[:, p * 2 * FACE : (p + 1) * 2 * FACE]
            b = upper[:, p * 2 * FACE : (p + 1) * 2 * FACE]
            if odd:
                a = pltpu.roll(a, FACE, 1)
            else:
                b = pltpu.roll(b, FACE, 1)
            blocks.append(jnp.where(low_half, a, b))
        return split(jnp.concatenate(blocks, axis=0))

    def stage(step, carry):
        trace = lame * (w[3] + w[4] + w[5])
        fields = [2.0 * (shear * w[3 + k]) + trace for k in range(3)]
        fields += [shear * w[6 + k] for k in range(3)]
        fields += [density * w[k] for k in range(3)]
        for k in range(9):
            high, low = split(fields[k])
            xh[k * e : (k + 1) * e, :] = high
            xl[k * e : (k + 1) * e, :] = low
        put_trace(1, e1)

        @pl.when(step == 0)
        def _():
            pl.semaphore_wait(barrier, 1 + n_seg)

        copies = send_side(step, 1)
        cd = comps(0)
        for p in range(3):
            a, b = fields[cd[2 * p]], fields[cd[2 * p + 1]]
            near = jnp.where(low_half, a[:, : 2 * FACE], pltpu.roll(b[:, : 2 * FACE], FACE, 1))
            far = jnp.where(low_half, pltpu.roll(a[:, -2 * FACE :], FACE, 1), b[:, -2 * FACE :])
            for s, value in ((0, near), (1, far)):
                high, low = split(value)
                cols = slice(p * 2 * FACE, (p + 1) * 2 * FACE)
                table[s * e : (s + 1) * e, cols] = high
                table[faces + s * e : faces + (s + 1) * e, cols] = low
        copies += send_side(step, 0)

        @pl.when(step == 0)
        def _():
            for k in early[1:2] + early[3:]:
                loads[k].wait()

        before = jnp.where(step == 0, 0.0, share(step - 1)).astype(F32)
        for k in range(9):
            out[k] = out[k] + before * vol[k]

        put_trace(2, e2)
        near = dot(pick[...], table[...])
        side = [near[f * e : (f + 1) * e, :] for f in range(6)]
        ahead = jnp.where(step < 2, 0.5 * STEP, STEP).astype(F32)
        seen = set()
        for d in range(3):
            cd = comps(d)
            high = jnp.concatenate([xh[c * e : (c + 1) * e, :] for c in cd], axis=0)
            low = jnp.concatenate([xl[c * e : (c + 1) * e, :] for c in cd], axis=0)
            if d == 0:
                parts = [dot(jnp.concatenate([high, low, high], axis=1), d0[...])]
            else:
                parts = []
                spread = (None, s1, s2)[d]
                face_high, face_low = face_rows(side[2 * d], side[2 * d + 1])
                for h in range(2):
                    a = high[:, h * HALF : (h + 1) * HALF]
                    b = low[:, h * HALF : (h + 1) * HALF]
                    left = jnp.concatenate([a, b, a, face_high, face_low], axis=1)
                    right = [derivs[d][...], spread[:, h * HALF : (h + 1) * HALF]]
                    parts.append(dot(left, jnp.concatenate(right, axis=0)))
            width = NODES // len(parts)
            for c, row in enumerate(rows(d)):
                for h, part in enumerate(parts):
                    piece = part[c * e : (c + 1) * e, :]
                    cols = slice(h * width, (h + 1) * width)
                    if row in seen:
                        vol[row, :, cols] += piece
                    else:
                        vol[row, :, cols] = piece
                seen.add(row)
        for row, (a, b) in zip(rows(0), onto_first(side[0], side[1])):
            vol[row, :, : 2 * FACE] += a
            vol[row, :, -2 * FACE :] += b
        for k in range(9):
            w[k] = adj[k] + ahead * vol[k]

        def far(d):
            for copy in copies[2 - 2 * d : 4 - 2 * d]:
                copy.wait()
            got = inbox[step, 2 * d : 2 * d + 2].reshape(pair, 6 * FACE)
            high, low = split(got)
            far_table[d, :pair, :] = high
            far_table[d, pair:, :] = low
            picked = dot(far_pick[2 * d * e : 2 * (d + 1) * e, :], far_table[d])
            return picked[:e], picked[e:]

        for row, (a, b) in zip(rows(0), onto_first(*far(0))):
            vol[row, :, : 2 * FACE] += a
            vol[row, :, -2 * FACE :] += b
            w[row, :, : 2 * FACE] += ahead * a
            w[row, :, -2 * FACE :] += ahead * b
        lifted = dot(jnp.concatenate(face_rows(*far(1)), axis=1), s1[...])
        for c, row in enumerate(rows(1)):
            piece = lifted[c * e : (c + 1) * e, :]
            vol[row] += piece
            w[row] += ahead * piece
        return carry

    lax.fori_loop(0, 4, stage, 0)
    for k in range(9):
        out[k] = out[k] + (STEP / 6.0) * vol[k]
    for k in (8, 9, 10):
        loads[k].wait()

    own = si.astype(F32)
    kids = mig[...].astype(F32)
    owner, slot, octant = kids[0:1, :], kids[1:2, :], kids[2:3, :]
    key = jnp.where(owner == own, slot, parents + owner * SLOTS + slot)
    key_col = column(key, e)
    before = jnp.where(key_col < jnp.broadcast_to(key, (e, e)), 1.0, 0.0)
    rank = jnp.sum(before, axis=0, keepdims=True) * 0.125
    rank_col = column(rank, e)
    place = octant * parents + rank
    perm = jnp.where(iota((e, e), 0).astype(F32) == jnp.broadcast_to(place, (e, e)), 1.0, 0.0)
    perm = perm.astype(BF16)
    perm = jnp.concatenate([perm, perm], axis=1)
    quarter = e // 2
    ordered = []
    for k in range(9):
        high, low = split(out[k])
        ordered.append(dot(perm, jnp.concatenate([high, low], axis=0)))

    def fold(values, matrix, blocks):
        pairs = [[], []]
        for v in values:
            count = v.shape[0] // parents
            for bit in range(2):
                for c in range(bit, count, 2):
                    pairs[bit].append(v[c * parents : (c + 1) * parents, :])
        sides2 = [split(jnp.concatenate(p, axis=0)) for p in pairs]
        width = NODES // blocks
        results = []
        for h in range(blocks):
            cols = slice(h * width, (h + 1) * width)
            high = jnp.concatenate([s[0][:, cols] for s in sides2], axis=1)
            low = jnp.concatenate([s[1][:, cols] for s in sides2], axis=1)
            results.append(dot(jnp.concatenate([high, low, high], axis=1), matrix[...]))
        total = results[0] if blocks == 1 else jnp.concatenate(results, axis=1)
        m = total.shape[0] // 9
        return [total[k * m : (k + 1) * m, :] for k in range(9)]

    sums = fold(fold(fold(ordered, r2, 2), r1, 2), r0, 1)
    tiles = NODES // 128
    stacked = jnp.concatenate(
        [
            jnp.concatenate([s[:, k * 128 : (k + 1) * 128] for s in sums], axis=1)
            for k in range(tiles)
        ],
        axis=0,
    )
    zh, zl = split(stacked)
    groups2 = jnp.concatenate([zh, zl], axis=0)
    wide = 2 * tiles * parents
    lane = iota((e, wide), 1)
    member = rank_col == (lane % parents).astype(F32)
    group_key = jnp.sum(jnp.where(member, key_col, 0.0), axis=0, keepdims=True) * 0.125
    chunk = SLOTS * tiles
    total_rows = n_seg * chunk
    row = iota((total_rows, wide), 0)
    col = iota((total_rows, wide), 1)
    wanted = (parents + row // tiles).astype(F32)
    match = jnp.where(wanted == jnp.broadcast_to(group_key, (total_rows, wide)), 1.0, 0.0)
    same = (row % tiles) == (col // parents) % tiles
    chooser = jnp.where(same, match, 0.0).astype(BF16)
    pay[...] = dot(chooser, groups2).reshape(n_seg, chunk, 9 * 128)
    arrived[pl.ds(si, 1)] = jnp.zeros((1, chunk, 9 * 128), F32)
    moves = []
    for k in range(1, n_seg):
        to = lax.rem(si + k, n_seg)
        move = pltpu.make_async_remote_copy(
            src_ref=pay.at[to],
            dst_ref=arrived.at[si],
            send_sem=mig_send.at[k - 1],
            recv_sem=mig_recv.at[k - 1],
            device_id=(ci, to),
            device_id_type=MESH,
        )
        move.start()
        moves.append(move)

    nrow = tiles * parents
    family = child[...].astype(F32)
    holder = column(family[0:1, :], nrow)
    fslot = jnp.maximum(column(family[1:2, :], nrow), 0.0)
    at_home = holder == own
    r = iota((nrow, wide), 0)
    c = iota((nrow, wide), 1)
    home = (r % parents).astype(F32) == jnp.broadcast_to(group_key, (nrow, wide))
    home = jnp.where(home, 1.0, 0.0) * jnp.where(at_home, 1.0, 0.0)
    home = jnp.where(r // parents == (c // parents) % tiles, home, 0.0).astype(BF16)
    r = iota((nrow, total_rows), 0)
    c = iota((nrow, total_rows), 1)
    source = (holder * SLOTS + fslot) == (c // tiles).astype(F32)
    far = jnp.where(source, 1.0, 0.0) * jnp.where(at_home, 0.0, 1.0)
    far = jnp.where(r // parents == c % tiles, far, 0.0).astype(BF16)
    local = dot(home, groups2)
    for move in moves:
        move.wait()
    ah, al = split(arrived[...].reshape(total_rows, 9 * 128))
    result = local + dot(jnp.concatenate([far, far], axis=1), jnp.concatenate([ah, al], axis=0))
    for k in range(9):
        for t in range(tiles):
            par[k, :, t * 128 : (t + 1) * 128] = result[
                t * parents : (t + 1) * parents, k * 128 : (k + 1) * 128
            ]


def hand_over(a_in, b_in, a_out, b_out, sems):
    copies = [
        pltpu.make_async_copy(a_in, a_out, sems.at[0]),
        pltpu.make_async_copy(b_in, b_out, sems.at[1]),
    ]
    for copy in copies:
        copy.start()
    for copy in copies:
        copy.wait()


def shards(n_curve, n_seg, adjoint, material, face_partner, send_faces, migration, children):
    e = adjoint.shape[1]
    cap = send_faces.shape[2]
    parents = children.shape[1]
    tables = [jnp.asarray(m) for m in constants()]
    faces, pair = 6 * e, 2 * cap
    chunk = SLOTS * (NODES // 128)
    vmem = pl.BlockSpec(memory_space=pltpu.VMEM)
    away = pl.BlockSpec(memory_space=pl.ANY)
    dma = pltpu.SemaphoreType.DMA
    shapes = (
        jax.ShapeDtypeStruct((9, e, NODES), F32),
        jax.ShapeDtypeStruct((9, parents, NODES), F32),
    )
    results = pl.pallas_call(
        functools.partial(kernel, n_curve, n_seg, e, cap, parents),
        out_shape=tuple(pltpu.VMEM(x.shape, F32) for x in shapes),
        in_specs=[vmem] * 5 + [away] * (1 + len(tables)),
        out_specs=(vmem, vmem),
        scratch_shapes=[pltpu.VMEM((9, e, NODES), F32)]
        + [pltpu.VMEM(m.shape, BF16) for m in tables]
        + [
            pltpu.VMEM((9, e, NODES), F32),
            pltpu.VMEM((9 * e, NODES), BF16),
            pltpu.VMEM((9 * e, NODES), BF16),
            pltpu.VMEM((9, e, NODES), F32),
            pltpu.VMEM((2 * faces, 6 * FACE), BF16),
            pltpu.VMEM((2, 2 * pair, 6 * FACE), BF16),
            pltpu.VMEM((faces, 2 * faces), BF16),
            pltpu.VMEM((4 * e, 2 * pair), BF16),
            pltpu.VMEM((2 * pair, 4 * e), BF16),
            pltpu.VMEM((4, 4, cap, 6 * FACE), F32),
            pltpu.VMEM((4, 4, cap, 6 * FACE), F32),
            pltpu.VMEM((n_seg, chunk, 9 * 128), F32),
            pltpu.VMEM((n_seg, chunk, 9 * 128), F32),
            dma((13,)),
            dma((4, 4)),
            dma((4, 4)),
            dma((n_seg - 1,)),
            dma((n_seg - 1,)),
        ],
        compiler_params=pltpu.CompilerParams(
            collective_id=0, has_side_effects=True, vmem_limit_bytes=60 * 2**20
        ),
    )(material, face_partner.T, send_faces, migration, children, adjoint, *tables)
    return pl.pallas_call(
        hand_over,
        out_shape=shapes,
        in_specs=[vmem, vmem],
        out_specs=(away, away),
        scratch_shapes=[dma((2,))],
    )(*(pltpu.with_memory_space_constraint(x, pltpu.VMEM) for x in results))


def solution(mesh):
    both = ("curve", "seg")
    in_specs = (
        P(None, both, None),
        P(None, both),
        P(both, None),
        P(both, None, None),
        P(None, both),
        P(None, both),
    )
    out_specs = (P(None, both, None), P(None, both, None))
    body = functools.partial(shards, mesh.shape["curve"], mesh.shape["seg"])
    return jax.shard_map(
        body, mesh=mesh, in_specs=in_specs, out_specs=out_specs, check_vma=False
    )
```

```python
import functools

import jax
import jax.numpy as jnp
import numpy as np
from jax import lax
from jax.experimental import pallas as pl
from jax.experimental.pallas import tpu as pltpu
from jax.sharding import PartitionSpec as P

V = ((3, 8, 7), (8, 4, 6), (7, 6, 5))
F32 = jnp.float32
BF16 = jnp.bfloat16
NP = 8
NODES = NP**3
FACE = NP**2
HALF = NODES // 2
STEP = 0.8 / NP**2
GAIN = 0.5 * 0.5 * NP * (NP - 1)
SLOTS = 2


def lobatto_nodes():
    return -np.cos(np.pi * np.arange(NP) / (NP - 1))


def derivative_line():
    points = lobatto_nodes()
    ids = np.arange(NP)
    weight = np.where((ids == 0) | (ids == NP - 1), 2.0, 1.0)
    row, col = ids[:, None], ids[None, :]
    gap = np.where(row == col, 1.0, points[:, None] - points[None, :])
    matrix = weight[:, None] / weight[None, :] * (-1.0) ** (row + col) / gap
    matrix = np.where(row == col, 0.0, matrix)
    return matrix - np.eye(NP) * matrix.sum(axis=1)[:, None]


def refine_line(upper):
    points = lobatto_nodes()
    targets = (points + (2.0 * upper - 1.0)) / 2.0
    columns = []
    for column in range(NP):
        factor = np.ones(NP)
        for other in range(NP):
            if other != column:
                factor = factor * (targets - points[other]) / (points[column] - points[other])
        columns.append(factor)
    return np.stack(columns, axis=1)


def two_parts(matrix):
    matrix = np.asarray(matrix, np.float32)
    high = matrix.astype(jnp.bfloat16)
    low = (matrix - high.astype(np.float32)).astype(jnp.bfloat16)
    return high, low


def three_deep(matrix):
    high, low = two_parts(matrix)
    return np.concatenate([high, high, low], axis=0)


def line_operators(line):
    return (
        np.kron(line, np.eye(FACE)),
        np.kron(np.kron(np.eye(4), line), np.eye(NP)),
        np.kron(np.eye(32), line),
    )


def constants():
    line = derivative_line()
    line[0, 0] += GAIN
    line[NP - 1, NP - 1] -= GAIN
    derivs = [three_deep(m) for m in line_operators(line)]
    lower = line_operators(refine_line(0))
    upper = line_operators(refine_line(1))
    refines = [three_deep(np.concatenate([a, b], axis=0)) for a, b in zip(lower, upper)]
    return derivs + refines


def split(x):
    high = x.astype(BF16)
    return high, (x - high.astype(F32)).astype(BF16)


def dot(a, b):
    return jnp.dot(a, b, preferred_element_type=F32)


def iota(shape, dim):
    return lax.broadcasted_iota(jnp.int32, shape, dim)


def column(row, count):
    n = row.shape[1]
    hit = iota((count, n), 0) % n == iota((count, n), 1)
    return jnp.sum(jnp.where(hit, jnp.broadcast_to(row, (count, n)), 0.0), axis=1, keepdims=True)


def kernel(
    n_curve, n_seg, e, cap, parents,
    mat, partner, send, mig, child, *refs
):
    hbm, refs = refs[:7], refs[7:]
    (
        out, par,
        adj, d0, d1, d2, r0, r1, r2,
        w, xh, xl, vol, table, far_table, pick, far_pick, sendpick,
        outbox, inbox, tie_out, tie_in, held, coef, late, echo, pay, arrived,
        load_sem, send_sem, recv_sem, tie_send, tie_recv, mig_send, mig_recv,
    ) = refs
    homes = (adj, d0, d1, d2, r0, r1, r2)
    loads = [
        pltpu.make_async_copy(hbm[k], homes[k], load_sem.at[k]) for k in range(len(homes))
    ]
    loads.append(pltpu.make_async_copy(hbm[0], w, load_sem.at[7]))
    early = (7, 0, 1, 2, 3)
    ci = lax.axis_index("curve")
    si = lax.axis_index("seg")
    cm = lax.rem(ci + n_curve - 1, n_curve)
    cp = lax.rem(ci + 1, n_curve)
    sm = lax.rem(si + n_seg - 1, n_seg)
    sp = lax.rem(si + 1, n_seg)
    sides = ((cm, si), (cp, si), (ci, sm), (ci, sp))
    barrier = pltpu.get_barrier_semaphore()
    MESH = pl.DeviceIdType.MESH
    for c in (cm, cp):
        pl.semaphore_signal(barrier, inc=1, device_id=(c, si), device_id_type=MESH)
    for k in range(1, n_seg):
        pl.semaphore_signal(
            barrier, inc=1, device_id=(ci, lax.rem(si + k, n_seg)), device_id_type=MESH
        )

    for k in early + (6, 5, 4):
        loads[k].start()

    faces = 6 * e
    pair = 2 * cap
    derivs = (d0, d1, d2)

    def codes(rows):
        k = iota((rows, faces), 1)
        return (6 * (k % e) + k // e).astype(F32)

    for r in range(4):
        k = iota((cap, 2 * e), 1)
        code = (6 * (k % e) + k // e + 2 * (r // 2)).astype(F32)
        want = column(send[0, r : r + 1, :].astype(F32), cap)
        hit = jnp.where(code == want, 1.0, 0.0).astype(BF16)
        sendpick[r * cap : (r + 1) * cap, :] = jnp.concatenate([hit, hit], axis=1)

    density = jnp.broadcast_to(1.0 / column(mat[0:1, :], e), (e, NODES))
    lame = jnp.broadcast_to(column(mat[1:2, :], e), (e, NODES))
    shear = jnp.broadcast_to(column(mat[2:3, :], e), (e, NODES))

    loads[early[0]].wait()
    low_half = iota((e, 2 * FACE), 1) < FACE

    def comps(d):
        return [V[d][0] - 3, V[d][1] - 3, V[d][2] - 3, 6, 7, 8]

    def rows(d):
        return [0, 1, 2, V[0][d], V[1][d], V[2][d]]

    lane = iota((e, 2 * FACE), 1)
    spot = lane % FACE
    group = spot // (2 * NP)

    def paths(d):
        stride = (None, 1, NP)[d]
        start = spot % (2 * NP) // NP * FACE + spot % NP * stride
        reach = FACE - NP if d == 1 else NP - 1
        return (
            start + jnp.where(low_half, 0, reach),
            start + jnp.where(low_half, reach, 0),
        )

    def gather(v, path):
        return jnp.take_along_axis(v, path, axis=1, mode="promise_in_bounds")

    def trace_pair(a, b, d):
        picks = []
        for v, path in zip((a, b), paths(d)):
            got = gather(v[:, : 2 * FACE], path)
            for j in range(1, 4):
                part = gather(v[:, j * 2 * FACE : (j + 1) * 2 * FACE], path)
                got = jnp.where(group == j, part, got)
            picks.append(got)
        a, b = picks
        return jnp.where(low_half, a, b), pltpu.roll(jnp.where(low_half, b, a), FACE, 1)

    def lift_paths(d):
        along = lane % FACE // NP if d == 1 else lane % NP
        across = lane % NP if d == 1 else lane % FACE // NP
        back = lane // FACE * NP + across
        gain = jnp.where(along == 0, GAIN, jnp.where(along == NP - 1, -GAIN, 0.0))
        starts = [
            jnp.where(along == NP - 1, FACE, 0) + j * 2 * NP + back for j in range(4)
        ]
        return starts, gain.astype(F32)

    def lift(v, d):
        starts, gain = lift_paths(d)
        return jnp.concatenate([gather(v, path) * gain for path in starts], axis=1)

    def face_copy(step, r):
        return pltpu.make_async_remote_copy(
            src_ref=outbox.at[step, r],
            dst_ref=inbox.at[step, r ^ 1],
            send_sem=send_sem.at[step, r],
            recv_sem=recv_sem.at[step, r ^ 1],
            device_id=sides[r],
            device_id_type=MESH,
        )

    def tie_copy(r):
        return pltpu.make_async_remote_copy(
            src_ref=tie_out.at[r - 2],
            dst_ref=tie_in.at[(r ^ 1) - 2],
            send_sem=tie_send.at[r - 2],
            recv_sem=tie_recv.at[(r ^ 1) - 2],
            device_id=sides[r],
            device_id_type=MESH,
        )

    def send_side(step, d, source):
        picked = dot(sendpick[d * pair : (d + 1) * pair, :], source)
        outbox[step, 2 * d : 2 * d + 2] = picked.reshape(2, cap, 6 * FACE)
        for r in (2 * d, 2 * d + 1):
            face_copy(step, r).start()

    def send_ahead(step):
        trace = lame * (w[3] + w[4] + w[5])
        images = [shear * w[V[1][k]] for k in range(3)]
        images[1] = 2.0 * images[1] + trace
        images += [density * w[k] for k in range(3)]
        pairs = [trace_pair(images[2 * p], images[2 * p + 1], 1) for p in range(3)]
        both = jnp.concatenate(
            [jnp.concatenate([p[s] for p in pairs], axis=1) for s in range(2)], axis=0
        )
        send_side(step, 1, jnp.concatenate(split(both), axis=0))
        held[...] = both

    def send_x(step):
        for s, cols in ((0, slice(0, 2 * FACE)), (1, slice(NODES - 2 * FACE, NODES))):
            mu, lam, rho = (v[:, : 2 * FACE] for v in (shear, lame, density))
            trace = lam * (w[3, :, cols] + w[4, :, cols] + w[5, :, cols])
            images = [mu * w[V[0][k], :, cols] for k in range(3)]
            images[0] = 2.0 * images[0] + trace
            images += [rho * w[k, :, cols] for k in range(3)]
            for p in range(3):
                a, b = images[2 * p], images[2 * p + 1]
                if s == 0:
                    value = jnp.where(low_half, a, pltpu.roll(b, FACE, 1))
                else:
                    value = jnp.where(low_half, pltpu.roll(a, FACE, 1), b)
                high, low = split(value)
                to = slice(p * 2 * FACE, (p + 1) * 2 * FACE)
                table[s * e : (s + 1) * e, to] = high
                table[faces + s * e : faces + (s + 1) * e, to] = low
        send_side(
            step,
            0,
            jnp.concatenate([table[: 2 * e, :], table[faces : faces + 2 * e, :]], axis=0),
        )

    def swap(v):
        n = v.shape[0]
        low = iota((n, 2 * FACE), 1) < FACE
        r = [pltpu.roll(v[:, k * 2 * FACE : (k + 1) * 2 * FACE], FACE, 1) for k in range(3)]
        return jnp.concatenate(
            [jnp.where(low, r[(k + 1) % 3], r[(k + 2) % 3]) for k in range(3)], axis=1
        )

    def onto_first(first, last):
        first, last = first * GAIN, last * -GAIN
        pieces = []
        for c in range(6):
            p, odd = c // 2, c % 2
            a = first[:, p * 2 * FACE : (p + 1) * 2 * FACE]
            b = last[:, p * 2 * FACE : (p + 1) * 2 * FACE]
            if odd:
                a = pltpu.roll(a, FACE, 1)
            else:
                b = pltpu.roll(b, FACE, 1)
            pieces.append((jnp.where(low_half, a, 0.0), jnp.where(low_half, 0.0, b)))
        return pieces

    def face_rows(lower, upper):
        blocks = []
        for c in range(6):
            p, odd = c // 2, c % 2
            a = lower[:, p * 2 * FACE : (p + 1) * 2 * FACE]
            b = upper[:, p * 2 * FACE : (p + 1) * 2 * FACE]
            if odd:
                a = pltpu.roll(a, FACE, 1)
            else:
                b = pltpu.roll(b, FACE, 1)
            blocks.append(jnp.where(low_half, a, b))
        return blocks

    narrow = [v[:, : 2 * FACE] for v in (density, lame, shear)]
    scale = jnp.concatenate(
        [
            jnp.where(low_half, narrow[2], 2.0 * narrow[2] + narrow[1]),
            jnp.where(low_half, narrow[2], narrow[0]),
            narrow[0],
        ],
        axis=1,
    )
    pl.semaphore_wait(barrier, 1 + n_seg)
    send_ahead(0)
    send_x(0)
    code = codes(e)
    wants = []
    for f in range(6):
        want = column(partner[f : f + 1, :].astype(F32), e)
        wants.append(want)
        hit = jnp.where(code == want, 1.0, 0.0).astype(BF16)
        pick[f * e : (f + 1) * e, :] = jnp.concatenate([hit, hit], axis=1)
        if f < 4:
            slot_code = (iota((e, pair), 1) + faces + (f // 2) * pair).astype(F32)
            far = jnp.where(slot_code == want, 1.0, 0.0).astype(BF16)
            far_pick[f * e : (f + 1) * e, :] = jnp.concatenate([far, far], axis=1)
    coef[:e, :] = GAIN * scale
    coef[e:, :] = -GAIN * scale
    ties = jnp.concatenate(
        [
            jnp.concatenate([GAIN * scale, jnp.broadcast_to(wants[2], (e, 2 * FACE))], axis=1),
            jnp.concatenate([-GAIN * scale, jnp.broadcast_to(wants[3], (e, 2 * FACE))], axis=1),
        ],
        axis=0,
    )
    picked = dot(sendpick[pair:, :], jnp.concatenate(split(ties), axis=0))
    tie_out[...] = picked.reshape(2, cap, 8 * FACE)
    for r in (2, 3):
        tie_copy(r).start()
    late[...] = jnp.zeros_like(late)
    for k in early[1:]:
        loads[k].wait()

    def three(picks, cols=slice(0, NODES)):
        high = jnp.concatenate([xh[c * e : (c + 1) * e, cols] for c in picks], axis=0)
        low = jnp.concatenate([xl[c * e : (c + 1) * e, cols] for c in picks], axis=0)
        return jnp.concatenate([high, low, high], axis=1)

    def stage(step, carry):
        trace = lame * (w[3] + w[4] + w[5])
        fields = [2.0 * (shear * w[3 + k]) + trace for k in range(3)]
        fields += [shear * w[6 + k] for k in range(3)]
        fields += [density * w[k] for k in range(3)]
        high, low = split(held[...])
        table[2 * e : 4 * e, :] = high
        table[faces + 2 * e : faces + 4 * e, :] = low
        for k in range(9):
            high, low = split(fields[k])
            xh[k * e : (k + 1) * e, :] = high
            xl[k * e : (k + 1) * e, :] = low

        part0 = dot(three(comps(0)), d0[...])
        keep = jnp.where(step == 0, -4.0 / 3.0, jnp.where(step == 2, 2.0 / 3.0, 1.0 / 3.0))
        keep = keep.astype(F32)
        for k in range(9):
            out[k] = jnp.where(step == 0, 0.0, out[k]) + keep * w[k]

        cd = comps(2)
        for p in range(3):
            cols = slice(p * 2 * FACE, (p + 1) * 2 * FACE)
            pair2 = trace_pair(fields[cd[2 * p]], fields[cd[2 * p + 1]], 2)
            for s, value in enumerate(pair2):
                high, low = split(value)
                table[(4 + s) * e : (5 + s) * e, cols] = high
                table[faces + (4 + s) * e : faces + (5 + s) * e, cols] = low
        near = dot(pick[...], table[...])
        side = [near[f * e : (f + 1) * e, :] for f in range(6)]
        ahead = jnp.where(step < 2, 0.5 * STEP, jnp.where(step == 2, STEP, STEP / 6.0))
        ahead = ahead.astype(F32)
        seen = set()
        for d in range(3):
            if d == 0:
                parts = [part0]
            else:
                lifts = [lift(v, d) for v in face_rows(side[2 * d], side[2 * d + 1])]
                parts = [
                    dot(three(comps(d), slice(h * HALF, (h + 1) * HALF)), derivs[d][...])
                    for h in range(2)
                ]
            width = NODES // len(parts)
            for c, row in enumerate(rows(d)):
                for h, part in enumerate(parts):
                    piece = part[c * e : (c + 1) * e, :]
                    cols = slice(h * width, (h + 1) * width)
                    if d > 0:
                        piece = piece + lifts[c][:, cols]
                    if row in seen:
                        vol[row, :, cols] += piece
                    else:
                        vol[row, :, cols] = piece
                seen.add(row)
        for row, (a, b) in zip(rows(0), onto_first(side[0], side[1])):
            vol[row, :, : 2 * FACE] += a
            vol[row, :, -2 * FACE :] += b
        for k in range(9):
            w[k] = adj[k] + ahead * vol[k]

        def far(d, got):
            high, low = split(got)
            far_table[d, :pair, :] = high
            far_table[d, pair:, :] = low
            return dot(far_pick[2 * d * e : 2 * (d + 1) * e, :], far_table[d])

        for r in (0, 1):
            face_copy(step, r).wait()
        picked = far(0, inbox[step, :2].reshape(pair, 6 * FACE))
        for row, (a, b) in zip(rows(0), onto_first(picked[:e], picked[e:])):
            w[row, :, : 2 * FACE] += ahead * a
            w[row, :, -2 * FACE :] += ahead * b

        @pl.when(step < 3)
        def _():
            send_ahead(step + 1)

        for r in (2, 3):
            face_copy(step, r).wait()
        got = inbox[step, 2:].reshape(pair, 6 * FACE) + late[...]
        picked = far(1, got)
        lifted = [lift(v, 1) for v in face_rows(picked[:e], picked[e:])]
        for piece, row in zip(lifted, rows(1)):
            w[row] += ahead * piece
        @pl.when(step < 3)
        def _():
            send_x(step + 1)

        held[...] = held[...] + ahead * (coef[...] * swap(picked))

        @pl.when(step == 0)
        def _():
            for r in (2, 3):
                tie_copy(r).wait()
            told = tie_in[:, :, 6 * FACE :].reshape(pair, 2 * FACE)[:, :pair]
            slot = iota((pair, pair), 1)
            mine = faces + (3 - slot // cap) * cap + slot % cap
            link = jnp.where(told == mine.astype(F32), 1.0, 0.0).astype(BF16)
            echo[...] = dot(link, sendpick[pair:, :]).astype(BF16)

        source = jnp.concatenate(
            [table[2 * e : 4 * e, :], table[faces + 2 * e : faces + 4 * e, :]], axis=0
        )
        ours = dot(echo[...], source)
        late[...] = ahead * (tie_in[:, :, : 6 * FACE].reshape(pair, 6 * FACE) * swap(ours))
        return carry

    lax.fori_loop(0, 4, stage, 0)
    for k in range(9):
        out[k] = out[k] + w[k]
    for k in (4, 5, 6):
        loads[k].wait()

    own = si.astype(F32)
    kids = mig[...].astype(F32)
    owner, slot, octant = kids[0:1, :], kids[1:2, :], kids[2:3, :]
    key = jnp.where(owner == own, slot, parents + owner * SLOTS + slot)
    key_col = column(key, e)
    before = jnp.where(key_col < jnp.broadcast_to(key, (e, e)), 1.0, 0.0)
    rank = jnp.sum(before, axis=0, keepdims=True) * 0.125
    rank_col = column(rank, e)
    place = octant * parents + rank
    perm = jnp.where(iota((e, e), 0).astype(F32) == jnp.broadcast_to(place, (e, e)), 1.0, 0.0)
    perm = perm.astype(BF16)
    perm = jnp.concatenate([perm, perm], axis=1)
    quarter = e // 2
    ordered = []
    for k in range(9):
        high, low = split(out[k])
        ordered.append(dot(perm, jnp.concatenate([high, low], axis=0)))

    def fold(values, matrix, blocks):
        pairs = [[], []]
        for v in values:
            count = v.shape[0] // parents
            for bit in range(2):
                for c in range(bit, count, 2):
                    pairs[bit].append(v[c * parents : (c + 1) * parents, :])
        sides2 = [split(jnp.concatenate(p, axis=0)) for p in pairs]
        width = NODES // blocks
        results = []
        for h in range(blocks):
            cols = slice(h * width, (h + 1) * width)
            high = jnp.concatenate([s[0][:, cols] for s in sides2], axis=1)
            low = jnp.concatenate([s[1][:, cols] for s in sides2], axis=1)
            results.append(dot(jnp.concatenate([high, low, high], axis=1), matrix[...]))
        total = results[0] if blocks == 1 else jnp.concatenate(results, axis=1)
        m = total.shape[0] // 9
        return [total[k * m : (k + 1) * m, :] for k in range(9)]

    sums = fold(fold(fold(ordered, r2, 2), r1, 2), r0, 1)
    tiles = NODES // 128
    stacked = jnp.concatenate(
        [
            jnp.concatenate([s[:, k * 128 : (k + 1) * 128] for s in sums], axis=1)
            for k in range(tiles)
        ],
        axis=0,
    )
    zh, zl = split(stacked)
    groups2 = jnp.concatenate([zh, zl], axis=0)
    wide = 2 * tiles * parents
    lane = iota((e, wide), 1)
    member = rank_col == (lane % parents).astype(F32)
    group_key = jnp.sum(jnp.where(member, key_col, 0.0), axis=0, keepdims=True) * 0.125
    chunk = SLOTS * tiles
    total_rows = n_seg * chunk
    row = iota((total_rows, wide), 0)
    col = iota((total_rows, wide), 1)
    wanted = (parents + row // tiles).astype(F32)
    match = jnp.where(wanted == jnp.broadcast_to(group_key, (total_rows, wide)), 1.0, 0.0)
    same = (row % tiles) == (col // parents) % tiles
    chooser = jnp.where(same, match, 0.0).astype(BF16)
    pay[...] = dot(chooser, groups2).reshape(n_seg, chunk, 9 * 128)
    arrived[pl.ds(si, 1)] = jnp.zeros((1, chunk, 9 * 128), F32)
    moves = []
    for k in range(1, n_seg):
        to = lax.rem(si + k, n_seg)
        move = pltpu.make_async_remote_copy(
            src_ref=pay.at[to],
            dst_ref=arrived.at[si],
            send_sem=mig_send.at[k - 1],
            recv_sem=mig_recv.at[k - 1],
            device_id=(ci, to),
            device_id_type=MESH,
        )
        move.start()
        moves.append(move)

    nrow = tiles * parents
    family = child[...].astype(F32)
    holder = column(family[0:1, :], nrow)
    fslot = jnp.maximum(column(family[1:2, :], nrow), 0.0)
    at_home = holder == own
    r = iota((nrow, wide), 0)
    c = iota((nrow, wide), 1)
    home = (r % parents).astype(F32) == jnp.broadcast_to(group_key, (nrow, wide))
    home = jnp.where(home, 1.0, 0.0) * jnp.where(at_home, 1.0, 0.0)
    home = jnp.where(r // parents == (c // parents) % tiles, home, 0.0).astype(BF16)
    r = iota((nrow, total_rows), 0)
    c = iota((nrow, total_rows), 1)
    source = (holder * SLOTS + fslot) == (c // tiles).astype(F32)
    far = jnp.where(source, 1.0, 0.0) * jnp.where(at_home, 0.0, 1.0)
    far = jnp.where(r // parents == c % tiles, far, 0.0).astype(BF16)
    local = dot(home, groups2)
    for move in moves:
        move.wait()
    ah, al = split(arrived[...].reshape(total_rows, 9 * 128))
    result = local + dot(jnp.concatenate([far, far], axis=1), jnp.concatenate([ah, al], axis=0))
    for k in range(9):
        for t in range(tiles):
            par[k, :, t * 128 : (t + 1) * 128] = result[
                t * parents : (t + 1) * parents, k * 128 : (k + 1) * 128
            ]


def hand_over(a_in, b_in, a_out, b_out, sems):
    copies = [
        pltpu.make_async_copy(a_in, a_out, sems.at[0]),
        pltpu.make_async_copy(b_in, b_out, sems.at[1]),
    ]
    for copy in copies:
        copy.start()
    for copy in copies:
        copy.wait()


def shards(n_curve, n_seg, adjoint, material, face_partner, send_faces, migration, children):
    e = adjoint.shape[1]
    cap = send_faces.shape[2]
    parents = children.shape[1]
    tables = [jnp.asarray(m) for m in constants()]
    faces, pair = 6 * e, 2 * cap
    chunk = SLOTS * (NODES // 128)
    vmem = pl.BlockSpec(memory_space=pltpu.VMEM)
    away = pl.BlockSpec(memory_space=pl.ANY)
    dma = pltpu.SemaphoreType.DMA
    shapes = (
        jax.ShapeDtypeStruct((9, e, NODES), F32),
        jax.ShapeDtypeStruct((9, parents, NODES), F32),
    )
    results = pl.pallas_call(
        functools.partial(kernel, n_curve, n_seg, e, cap, parents),
        out_shape=tuple(pltpu.VMEM(x.shape, F32) for x in shapes),
        in_specs=[vmem] * 5 + [away] * (1 + len(tables)),
        out_specs=(vmem, vmem),
        scratch_shapes=[pltpu.VMEM((9, e, NODES), F32)]
        + [pltpu.VMEM(m.shape, BF16) for m in tables]
        + [
            pltpu.VMEM((9, e, NODES), F32),
            pltpu.VMEM((9 * e, NODES), BF16),
            pltpu.VMEM((9 * e, NODES), BF16),
            pltpu.VMEM((9, e, NODES), F32),
            pltpu.VMEM((2 * faces, 6 * FACE), BF16),
            pltpu.VMEM((2, 2 * pair, 6 * FACE), BF16),
            pltpu.VMEM((faces, 2 * faces), BF16),
            pltpu.VMEM((4 * e, 2 * pair), BF16),
            pltpu.VMEM((2 * pair, 4 * e), BF16),
            pltpu.VMEM((4, 4, cap, 6 * FACE), F32),
            pltpu.VMEM((4, 4, cap, 6 * FACE), F32),
            pltpu.VMEM((2, cap, 8 * FACE), F32),
            pltpu.VMEM((2, cap, 8 * FACE), F32),
            pltpu.VMEM((2 * e, 6 * FACE), F32),
            pltpu.VMEM((2 * e, 6 * FACE), F32),
            pltpu.VMEM((pair, 6 * FACE), F32),
            pltpu.VMEM((pair, 4 * e), BF16),
            pltpu.VMEM((n_seg, chunk, 9 * 128), F32),
            pltpu.VMEM((n_seg, chunk, 9 * 128), F32),
            dma((8,)),
            dma((4, 4)),
            dma((4, 4)),
            dma((2,)),
            dma((2,)),
            dma((n_seg - 1,)),
            dma((n_seg - 1,)),
        ],
        compiler_params=pltpu.CompilerParams(
            collective_id=0, has_side_effects=True, vmem_limit_bytes=60 * 2**20
        ),
    )(material, face_partner.T, send_faces, migration, children, adjoint, *tables)
    return pl.pallas_call(
        hand_over,
        out_shape=shapes,
        in_specs=[vmem, vmem],
        out_specs=(away, away),
        scratch_shapes=[dma((2,))],
    )(*(pltpu.with_memory_space_constraint(x, pltpu.VMEM) for x in results))


def solution(mesh):
    both = ("curve", "seg")
    in_specs = (
        P(None, both, None),
        P(None, both),
        P(both, None),
        P(both, None, None),
        P(None, both),
        P(None, both),
    )
    out_specs = (P(None, both, None), P(None, both, None))
    body = functools.partial(shards, mesh.shape["curve"], mesh.shape["seg"])
    return jax.shard_map(
        body, mesh=mesh, in_specs=in_specs, out_specs=out_specs, check_vma=False
    )
```

```python
import functools

import jax
import jax.numpy as jnp
import numpy as np
from jax import lax
from jax.experimental import pallas as pl
from jax.experimental.pallas import tpu as pltpu
from jax.sharding import PartitionSpec as P

V = ((3, 8, 7), (8, 4, 6), (7, 6, 5))
F32 = jnp.float32
BF16 = jnp.bfloat16
NP = 8
NODES = NP**3
FACE = NP**2
HALF = NODES // 2
STEP = 0.8 / NP**2
GAIN = 0.5 * 0.5 * NP * (NP - 1)
SLOTS = 2
GROUPS = 1


def lobatto_nodes():
    return -np.cos(np.pi * np.arange(NP) / (NP - 1))


def derivative_line():
    points = lobatto_nodes()
    ids = np.arange(NP)
    weight = np.where((ids == 0) | (ids == NP - 1), 2.0, 1.0)
    row, col = ids[:, None], ids[None, :]
    gap = np.where(row == col, 1.0, points[:, None] - points[None, :])
    matrix = weight[:, None] / weight[None, :] * (-1.0) ** (row + col) / gap
    matrix = np.where(row == col, 0.0, matrix)
    return matrix - np.eye(NP) * matrix.sum(axis=1)[:, None]


def refine_line(upper):
    points = lobatto_nodes()
    targets = (points + (2.0 * upper - 1.0)) / 2.0
    columns = []
    for column in range(NP):
        factor = np.ones(NP)
        for other in range(NP):
            if other != column:
                factor = factor * (targets - points[other]) / (points[column] - points[other])
        columns.append(factor)
    return np.stack(columns, axis=1)


def two_parts(matrix):
    matrix = np.asarray(matrix, np.float32)
    high = matrix.astype(jnp.bfloat16)
    low = (matrix - high.astype(np.float32)).astype(jnp.bfloat16)
    return high, low


def three_deep(matrix):
    high, low = two_parts(matrix)
    return np.concatenate([high, high, low], axis=0)


def line_operators(line):
    return (
        np.kron(line, np.eye(FACE)),
        np.kron(np.kron(np.eye(4), line), np.eye(NP)),
        np.kron(np.eye(32), line),
    )


def constants():
    line = derivative_line()
    line[0, 0] += GAIN
    line[NP - 1, NP - 1] -= GAIN
    derivs = [three_deep(m) for m in line_operators(line)]
    halves = [line_operators(refine_line(b)) for b in range(2)]
    quads = [
        halves[k // 2][1] @ halves[k % 2][2] for k in range(4)
    ]
    refines = [
        three_deep(np.concatenate([halves[0][0], halves[1][0]], axis=0)),
        three_deep(np.concatenate(quads, axis=0)),
    ]
    return derivs + refines


def split(x):
    high = x.astype(BF16)
    return high, (x - high.astype(F32)).astype(BF16)


def dot(a, b):
    return jnp.dot(a, b, preferred_element_type=F32)


def iota(shape, dim):
    return lax.broadcasted_iota(jnp.int32, shape, dim)


def column(row, count):
    n = row.shape[1]
    hit = iota((count, n), 0) % n == iota((count, n), 1)
    return jnp.sum(jnp.where(hit, jnp.broadcast_to(row, (count, n)), 0.0), axis=1, keepdims=True)


def kernel(
    n_curve, n_seg, e, cap, parents,
    *refs
):
    given, hbm, refs = refs[:5], refs[5:11], refs[11:]
    (
        out, par,
        mat, partner, send, mig, child,
        adj, d0, d1, d2, r0, r1,
        w, xh, xl, vol, table, far_table, pick, far_pick, sendpick,
        outbox, inbox, tie_out, tie_in, held, coef, late, echo, pay, arrived,
        small_sem, load_sem, send_sem, recv_sem, tie_send, tie_recv, mig_send, mig_recv,
    ) = refs
    homes = (adj, d0, d1, d2, r0, r1)
    loads = [
        pltpu.make_async_copy(hbm[k], homes[k], load_sem.at[k]) for k in range(len(homes))
    ]
    loads.append(pltpu.make_async_copy(hbm[0], w, load_sem.at[6]))
    early = (6, 0, 1, 2, 3)
    small = [
        pltpu.make_async_copy(a, b, small_sem.at[k])
        for k, (a, b) in enumerate(zip(given, (mat, send, partner, mig, child)))
    ]
    for copy in small[:2]:
        copy.start()
    loads[early[0]].start()
    for copy in small[2:]:
        copy.start()
    for k in early[1:] + (5, 4):
        loads[k].start()
    ci = lax.axis_index("curve")
    si = lax.axis_index("seg")
    cm = lax.rem(ci + n_curve - 1, n_curve)
    cp = lax.rem(ci + 1, n_curve)
    sm = lax.rem(si + n_seg - 1, n_seg)
    sp = lax.rem(si + 1, n_seg)
    sides = ((cm, si), (cp, si), (ci, sm), (ci, sp))
    barrier = pltpu.get_barrier_semaphore()
    MESH = pl.DeviceIdType.MESH
    for c in (cm, cp):
        pl.semaphore_signal(barrier, inc=1, device_id=(c, si), device_id_type=MESH)
    for k in range(1, n_seg):
        pl.semaphore_signal(
            barrier, inc=1, device_id=(ci, lax.rem(si + k, n_seg)), device_id_type=MESH
        )


    faces = 6 * e
    pair = 2 * cap
    small[1].wait()
    derivs = (d0, d1, d2)

    def codes(rows):
        k = iota((rows, faces), 1)
        return (6 * (k % e) + k // e).astype(F32)

    for r in range(4):
        k = iota((cap, 2 * e), 1)
        code = (6 * (k % e) + k // e + 2 * (r // 2)).astype(F32)
        want = column(send[0, r : r + 1, :].astype(F32), cap)
        hit = jnp.where(code == want, 1.0, 0.0).astype(BF16)
        sendpick[r * cap : (r + 1) * cap, :] = jnp.concatenate([hit, hit], axis=1)

    small[0].wait()
    density = jnp.broadcast_to(1.0 / column(mat[0:1, :], e), (e, NODES))
    lame = jnp.broadcast_to(column(mat[1:2, :], e), (e, NODES))
    shear = jnp.broadcast_to(column(mat[2:3, :], e), (e, NODES))

    loads[early[0]].wait()
    low_half = iota((e, 2 * FACE), 1) < FACE

    def comps(d):
        return [V[d][0] - 3, V[d][1] - 3, V[d][2] - 3, 6, 7, 8]

    def rows(d):
        return [0, 1, 2, V[0][d], V[1][d], V[2][d]]

    lane = iota((e, 2 * FACE), 1)
    spot = lane % FACE
    group = spot // (2 * NP)

    def paths(d):
        stride = (None, 1, NP)[d]
        start = spot % (2 * NP) // NP * FACE + spot % NP * stride
        reach = FACE - NP if d == 1 else NP - 1
        return (
            start + jnp.where(low_half, 0, reach),
            start + jnp.where(low_half, reach, 0),
        )

    def gather(v, path):
        return jnp.take_along_axis(v, path, axis=1, mode="promise_in_bounds")

    def trace_pair(a, b, d):
        picks = []
        for v, path in zip((a, b), paths(d)):
            got = gather(v[:, : 2 * FACE], path)
            for j in range(1, 4):
                part = gather(v[:, j * 2 * FACE : (j + 1) * 2 * FACE], path)
                got = jnp.where(group == j, part, got)
            picks.append(got)
        a, b = picks
        return jnp.where(low_half, a, b), pltpu.roll(jnp.where(low_half, b, a), FACE, 1)

    def lift_paths(d):
        along = lane % FACE // NP if d == 1 else lane % NP
        across = lane % NP if d == 1 else lane % FACE // NP
        back = lane // FACE * NP + across
        gain = jnp.where(along == 0, GAIN, jnp.where(along == NP - 1, -GAIN, 0.0))
        starts = [
            jnp.where(along == NP - 1, FACE, 0) + j * 2 * NP + back for j in range(4)
        ]
        return starts, gain.astype(F32)

    def lift(v, d):
        starts, gain = lift_paths(d)
        return jnp.concatenate([gather(v, path) * gain for path in starts], axis=1)

    def face_copy(step, r):
        return pltpu.make_async_remote_copy(
            src_ref=outbox.at[step, r],
            dst_ref=inbox.at[step, r ^ 1],
            send_sem=send_sem.at[step, r],
            recv_sem=recv_sem.at[step, r ^ 1],
            device_id=sides[r],
            device_id_type=MESH,
        )

    def tie_copy(r):
        return pltpu.make_async_remote_copy(
            src_ref=tie_out.at[r - 2],
            dst_ref=tie_in.at[(r ^ 1) - 2],
            send_sem=tie_send.at[r - 2],
            recv_sem=tie_recv.at[(r ^ 1) - 2],
            device_id=sides[r],
            device_id_type=MESH,
        )

    def send_side(step, d, source):
        picked = dot(sendpick[d * pair : (d + 1) * pair, :], source)
        outbox[step, 2 * d : 2 * d + 2] = picked.reshape(2, cap, 6 * FACE)
        for r in (2 * d, 2 * d + 1):
            face_copy(step, r).start()

    def y_faces():
        trace = lame * (w[3] + w[4] + w[5])
        images = [shear * w[V[1][k]] for k in range(3)]
        images[1] = 2.0 * images[1] + trace
        images += [density * w[k] for k in range(3)]
        pairs = [trace_pair(images[2 * p], images[2 * p + 1], 1) for p in range(3)]
        return jnp.concatenate(
            [jnp.concatenate([p[s] for p in pairs], axis=1) for s in range(2)], axis=0
        )

    def x_faces():
        sides2 = []
        for s, cols in ((0, slice(0, 2 * FACE)), (1, slice(NODES - 2 * FACE, NODES))):
            rho, lam, mu = narrow
            trace = lam * (w[3, :, cols] + w[4, :, cols] + w[5, :, cols])
            images = [mu * w[V[0][k], :, cols] for k in range(3)]
            images[0] = 2.0 * images[0] + trace
            images += [rho * w[k, :, cols] for k in range(3)]
            values = []
            for p in range(3):
                a, b = images[2 * p], images[2 * p + 1]
                if s == 0:
                    values.append(jnp.where(low_half, a, pltpu.roll(b, FACE, 1)))
                else:
                    values.append(jnp.where(low_half, pltpu.roll(a, FACE, 1), b))
            sides2.append(jnp.concatenate(values, axis=1))
        return jnp.concatenate(sides2, axis=0)

    def send_y(step, both):
        send_side(step, 1, jnp.concatenate(split(both), axis=0))
        held[...] = both

    def send_x(step, both):
        high, low = split(both)
        table[: 2 * e, :] = high
        table[faces : faces + 2 * e, :] = low
        send_side(step, 0, jnp.concatenate([high, low], axis=0))

    def edges(blocks, d):
        line, across = spot // NP, spot % NP
        path = jnp.where(line == NP - 1, FACE, 0) + jnp.where(low_half, 0, FACE - NP) + across
        gain = jnp.where(line == 0, GAIN, jnp.where(line == NP - 1, -GAIN, 0.0)).astype(F32)
        rho, lam, mu = (v * gain for v in narrow)
        u = [rho * gather(blocks[k], path) for k in range(3)]
        a, b = gather(blocks[3], path), gather(blocks[4], path)
        images = [lam * b, mu * a] if d == 0 else [mu * b, lam * a]
        return images + [None] + u

    def paired(images):
        sides2 = [[], []]
        for p in range(3):
            a, b = images[2 * p], images[2 * p + 1]
            if a is None:
                sides2[0].append(jnp.where(low_half, 0.0, pltpu.roll(b, FACE, 1)))
                sides2[1].append(jnp.where(low_half, 0.0, b))
            else:
                sides2[0].append(jnp.where(low_half, a, pltpu.roll(b, FACE, 1)))
                sides2[1].append(jnp.where(low_half, pltpu.roll(a, FACE, 1), b))
        return jnp.concatenate([jnp.concatenate(v, axis=1) for v in sides2], axis=0)

    def swap(v):
        n = v.shape[0]
        low = iota((n, 2 * FACE), 1) < FACE
        r = [pltpu.roll(v[:, k * 2 * FACE : (k + 1) * 2 * FACE], FACE, 1) for k in range(3)]
        return jnp.concatenate(
            [jnp.where(low, r[(k + 1) % 3], r[(k + 2) % 3]) for k in range(3)], axis=1
        )

    def onto_first(first, last):
        first, last = first * GAIN, last * -GAIN
        pieces = []
        for c in range(6):
            p, odd = c // 2, c % 2
            a = first[:, p * 2 * FACE : (p + 1) * 2 * FACE]
            b = last[:, p * 2 * FACE : (p + 1) * 2 * FACE]
            if odd:
                a = pltpu.roll(a, FACE, 1)
            else:
                b = pltpu.roll(b, FACE, 1)
            pieces.append((jnp.where(low_half, a, 0.0), jnp.where(low_half, 0.0, b)))
        return pieces

    def face_rows(lower, upper):
        blocks = []
        for c in range(6):
            p, odd = c // 2, c % 2
            a = lower[:, p * 2 * FACE : (p + 1) * 2 * FACE]
            b = upper[:, p * 2 * FACE : (p + 1) * 2 * FACE]
            if odd:
                a = pltpu.roll(a, FACE, 1)
            else:
                b = pltpu.roll(b, FACE, 1)
            blocks.append(jnp.where(low_half, a, b))
        return blocks

    narrow = [v[:, : 2 * FACE] for v in (density, lame, shear)]
    scale = jnp.concatenate(
        [
            jnp.where(low_half, narrow[2], 2.0 * narrow[2] + narrow[1]),
            jnp.where(low_half, narrow[2], narrow[0]),
            narrow[0],
        ],
        axis=1,
    )
    first = y_faces(), x_faces()
    pl.semaphore_wait(barrier, 1 + n_seg)
    send_y(0, first[0])
    send_x(0, first[1])
    code = codes(e)
    wants = []
    for copy in small[2:]:
        copy.wait()
    for f in range(6):
        want = column(partner[f : f + 1, :].astype(F32), e)
        wants.append(want)
        hit = jnp.where(code == want, 1.0, 0.0).astype(BF16)
        pick[f * e : (f + 1) * e, :] = jnp.concatenate([hit, hit], axis=1)
        if f < 4:
            slot_code = (iota((e, pair), 1) + faces + (f // 2) * pair).astype(F32)
            far = jnp.where(slot_code == want, 1.0, 0.0).astype(BF16)
            far_pick[f * e : (f + 1) * e, :] = jnp.concatenate([far, far], axis=1)
    coef[:e, :] = GAIN * scale
    coef[e:, :] = -GAIN * scale
    ties = jnp.concatenate(
        [
            jnp.concatenate([GAIN * scale, jnp.broadcast_to(wants[2], (e, 2 * FACE))], axis=1),
            jnp.concatenate([-GAIN * scale, jnp.broadcast_to(wants[3], (e, 2 * FACE))], axis=1),
        ],
        axis=0,
    )
    picked = dot(sendpick[pair:, :], jnp.concatenate(split(ties), axis=0))
    tie_out[...] = picked.reshape(2, cap, 8 * FACE)
    for r in (2, 3):
        tie_copy(r).start()
    late[...] = jnp.zeros_like(late)
    own = si.astype(F32)
    kids = mig[...].astype(F32)
    owner, slot, octant = kids[0:1, :], kids[1:2, :], kids[2:3, :]
    key = jnp.where(owner == own, slot, parents + owner * SLOTS + slot)
    key_col = column(key, e)
    earlier = jnp.where(key_col < jnp.broadcast_to(key, (e, e)), 1.0, 0.0)
    rank = jnp.sum(earlier, axis=0, keepdims=True) * 0.125
    rank_col = column(rank, e)
    place = octant * parents + rank
    perm = jnp.where(iota((e, e), 0).astype(F32) == jnp.broadcast_to(place, (e, e)), 1.0, 0.0)
    perm = perm.astype(BF16)
    perm = jnp.concatenate([perm, perm], axis=1)
    per = 9 // GROUPS
    tiles = NODES // 128
    wide = 2 * tiles * parents
    strip = iota((e, wide), 1)
    member = rank_col == (strip % parents).astype(F32)
    group_key = jnp.sum(jnp.where(member, key_col, 0.0), axis=0, keepdims=True) * 0.125
    chunk = SLOTS * tiles
    total_rows = n_seg * chunk
    row = iota((total_rows, wide), 0)
    col = iota((total_rows, wide), 1)
    wanted = (parents + row // tiles).astype(F32)
    match = jnp.where(wanted == jnp.broadcast_to(group_key, (total_rows, wide)), 1.0, 0.0)
    same = (row % tiles) == (col // parents) % tiles
    chooser = jnp.where(same, match, 0.0).astype(BF16)
    nrow = tiles * parents
    family = child[...].astype(F32)
    holder = column(family[0:1, :], nrow)
    fslot = jnp.maximum(column(family[1:2, :], nrow), 0.0)
    at_home = holder == own
    r = iota((nrow, wide), 0)
    c = iota((nrow, wide), 1)
    home = (r % parents).astype(F32) == jnp.broadcast_to(group_key, (nrow, wide))
    home = jnp.where(home, 1.0, 0.0) * jnp.where(at_home, 1.0, 0.0)
    home = jnp.where(r // parents == (c // parents) % tiles, home, 0.0).astype(BF16)
    r = iota((nrow, total_rows), 0)
    c = iota((nrow, total_rows), 1)
    source = (holder * SLOTS + fslot) == (c // tiles).astype(F32)
    away = jnp.where(source, 1.0, 0.0) * jnp.where(at_home, 0.0, 1.0)
    away = jnp.where(r // parents == c % tiles, away, 0.0).astype(BF16)
    for g in range(GROUPS):
        arrived[g, pl.ds(si, 1)] = jnp.zeros((1, chunk, per * 128), F32)
    for k in early[1:]:
        loads[k].wait()

    def three(picks, cols=slice(0, NODES)):
        high = jnp.concatenate([xh[c * e : (c + 1) * e, cols] for c in picks], axis=0)
        low = jnp.concatenate([xl[c * e : (c + 1) * e, cols] for c in picks], axis=0)
        return jnp.concatenate([high, low, high], axis=1)

    def stage(step, carry):
        trace = lame * (w[3] + w[4] + w[5])
        fields = [2.0 * (shear * w[3 + k]) + trace for k in range(3)]
        fields += [shear * w[6 + k] for k in range(3)]
        fields += [density * w[k] for k in range(3)]
        high, low = split(held[...])
        table[2 * e : 4 * e, :] = high
        table[faces + 2 * e : faces + 4 * e, :] = low
        for k in range(9):
            high, low = split(fields[k])
            xh[k * e : (k + 1) * e, :] = high
            xl[k * e : (k + 1) * e, :] = low

        part0 = dot(three(comps(0)), d0[...])
        keep = jnp.where(step == 0, -4.0 / 3.0, jnp.where(step == 2, 2.0 / 3.0, 1.0 / 3.0))
        keep = keep.astype(F32)
        for k in range(9):
            out[k] = jnp.where(step == 0, 0.0, out[k]) + keep * w[k]

        cd = comps(2)
        for p in range(3):
            cols = slice(p * 2 * FACE, (p + 1) * 2 * FACE)
            pair2 = trace_pair(fields[cd[2 * p]], fields[cd[2 * p + 1]], 2)
            for s, value in enumerate(pair2):
                high, low = split(value)
                table[(4 + s) * e : (5 + s) * e, cols] = high
                table[faces + (4 + s) * e : faces + (5 + s) * e, cols] = low
        near = dot(pick[...], table[...])
        side = [near[f * e : (f + 1) * e, :] for f in range(6)]
        ahead = jnp.where(step < 2, 0.5 * STEP, jnp.where(step == 2, STEP, STEP / 6.0))
        ahead = ahead.astype(F32)
        seen = set()
        for d in range(3):
            if d == 0:
                parts = [part0]
            else:
                lifts = [lift(v, d) for v in face_rows(side[2 * d], side[2 * d + 1])]
                parts = [
                    dot(three(comps(d), slice(h * HALF, (h + 1) * HALF)), derivs[d][...])
                    for h in range(2)
                ]
            width = NODES // len(parts)
            for c, row in enumerate(rows(d)):
                for h, part in enumerate(parts):
                    piece = part[c * e : (c + 1) * e, :]
                    cols = slice(h * width, (h + 1) * width)
                    if d > 0:
                        piece = piece + lifts[c][:, cols]
                    if row in seen:
                        vol[row, :, cols] += piece
                    else:
                        vol[row, :, cols] = piece
                seen.add(row)
        for row, (a, b) in zip(rows(0), onto_first(side[0], side[1])):
            vol[row, :, : 2 * FACE] += a
            vol[row, :, -2 * FACE :] += b
        for k in range(9):
            w[k] = adj[k] + ahead * vol[k]

        def far(d, got):
            high, low = split(got)
            far_table[d, :pair, :] = high
            far_table[d, pair:, :] = low
            return dot(far_pick[2 * d * e : 2 * (d + 1) * e, :], far_table[d])

        def arrive(d):
            for r in (2 * d, 2 * d + 1):
                face_copy(step, r).wait()
            got = inbox[step, 2 * d : 2 * d + 2].reshape(pair, 6 * FACE)
            if d == 1:
                got = got + late[...]
            picked = far(d, got)
            return picked, face_rows(picked[:e], picked[e:])

        def apply_x(picked):
            for row, (a, b) in zip(rows(0), onto_first(picked[:e], picked[e:])):
                w[row, :, : 2 * FACE] += ahead * a
                w[row, :, -2 * FACE :] += ahead * b

        def apply_y(blocks):
            for v, row in zip(blocks, rows(1)):
                w[row] += ahead * lift(v, 1)

        @pl.when(step < 3)
        def _():
            base = y_faces()
            picked, blocks = arrive(0)
            send_y(step + 1, base + ahead * paired(edges(blocks, 1)))
            apply_x(picked)
            base = x_faces()
            picked, blocks = arrive(1)
            source = jnp.concatenate(
                [table[2 * e : 4 * e, :], table[faces + 2 * e : faces + 4 * e, :]], axis=0
            )
            send_x(step + 1, base + ahead * paired(edges(blocks, 0)))
            apply_y(blocks)
            held[...] = held[...] + ahead * (coef[...] * swap(picked))

            @pl.when(step == 0)
            def _():
                for r in (2, 3):
                    tie_copy(r).wait()
                told = tie_in[:, :, 6 * FACE :].reshape(pair, 2 * FACE)[:, :pair]
                slot = iota((pair, pair), 1)
                mine = faces + (3 - slot // cap) * cap + slot % cap
                link = jnp.where(told == mine.astype(F32), 1.0, 0.0).astype(BF16)
                echo[...] = dot(link, sendpick[pair:, :]).astype(BF16)

            ours = dot(echo[...], source)
            late[...] = ahead * (tie_in[:, :, : 6 * FACE].reshape(pair, 6 * FACE) * swap(ours))

        @pl.when(step == 3)
        def _():
            apply_x(arrive(0)[0])
            apply_y(arrive(1)[1])

        return carry

    lax.fori_loop(0, 4, stage, 0)
    for k in (4, 5):
        loads[k].wait()

    def fold(values, matrix, ways, blocks):
        count = len(values)
        groups = [[] for _ in range(ways)]
        for v in values:
            octants = v.shape[0] // parents
            for way in range(ways):
                for c in range(way, octants, ways):
                    groups[way].append(v[c * parents : (c + 1) * parents, :])
        sides2 = [split(jnp.concatenate(p, axis=0)) for p in groups]
        width = NODES // blocks
        results = []
        for h in range(blocks):
            cols = slice(h * width, (h + 1) * width)
            high = jnp.concatenate([s[0][:, cols] for s in sides2], axis=1)
            low = jnp.concatenate([s[1][:, cols] for s in sides2], axis=1)
            results.append(dot(jnp.concatenate([high, low, high], axis=1), matrix[...]))
        total = results[0] if blocks == 1 else jnp.concatenate(results, axis=1)
        m = total.shape[0] // count
        return [total[k * m : (k + 1) * m, :] for k in range(count)]

    def migration_copy(g, k):
        to = lax.rem(si + k, n_seg)
        return pltpu.make_async_remote_copy(
            src_ref=pay.at[g, to],
            dst_ref=arrived.at[g, si],
            send_sem=mig_send.at[g, k - 1],
            recv_sem=mig_recv.at[g, k - 1],
            device_id=(ci, to),
            device_id_type=MESH,
        )

    local = []
    for g in range(GROUPS):
        ordered = []
        for k in range(g * per, (g + 1) * per):
            total = out[k] + w[k]
            out[k] = total
            ordered.append(dot(perm, jnp.concatenate(split(total), axis=0)))
        sums = fold(fold(ordered, r1, 4, 2), r0, 2, 1)
        stacked = jnp.concatenate(
            [
                jnp.concatenate([s[:, k * 128 : (k + 1) * 128] for s in sums], axis=1)
                for k in range(tiles)
            ],
            axis=0,
        )
        both = jnp.concatenate(split(stacked), axis=0)
        pay[g] = dot(chooser, both).reshape(n_seg, chunk, per * 128)
        for k in range(1, n_seg):
            migration_copy(g, k).start()
        local.append(dot(home, both))
    for g in range(GROUPS):
        for k in range(1, n_seg):
            migration_copy(g, k).wait()
        ah, al = split(arrived[g].reshape(total_rows, per * 128))
        result = local[g] + dot(
            jnp.concatenate([away, away], axis=1), jnp.concatenate([ah, al], axis=0)
        )
        for k in range(per):
            for t in range(tiles):
                par[g * per + k, :, t * 128 : (t + 1) * 128] = result[
                    t * parents : (t + 1) * parents, k * 128 : (k + 1) * 128
                ]


def hand_over(a_in, b_in, a_out, b_out, sems):
    copies = [
        pltpu.make_async_copy(a_in, a_out, sems.at[0]),
        pltpu.make_async_copy(b_in, b_out, sems.at[1]),
    ]
    for copy in copies:
        copy.start()
    for copy in copies:
        copy.wait()


def shards(n_curve, n_seg, adjoint, material, face_partner, send_faces, migration, children):
    e = adjoint.shape[1]
    cap = send_faces.shape[2]
    parents = children.shape[1]
    tables = [jnp.asarray(m) for m in constants()]
    faces, pair = 6 * e, 2 * cap
    chunk = SLOTS * (NODES // 128)
    vmem = pl.BlockSpec(memory_space=pltpu.VMEM)
    away = pl.BlockSpec(memory_space=pl.ANY)
    dma = pltpu.SemaphoreType.DMA
    shapes = (
        jax.ShapeDtypeStruct((9, e, NODES), F32),
        jax.ShapeDtypeStruct((9, parents, NODES), F32),
    )
    results = pl.pallas_call(
        functools.partial(kernel, n_curve, n_seg, e, cap, parents),
        out_shape=tuple(pltpu.VMEM(x.shape, F32) for x in shapes),
        in_specs=[away] * (6 + len(tables)),
        out_specs=(vmem, vmem),
        scratch_shapes=[
            pltpu.VMEM((3, e), F32),
            pltpu.VMEM((6, e), jnp.int32),
            pltpu.VMEM(send_faces.shape, jnp.int32),
            pltpu.VMEM((3, e), jnp.int32),
            pltpu.VMEM((2, parents), jnp.int32),
            pltpu.VMEM((9, e, NODES), F32),
        ]
        + [pltpu.VMEM(m.shape, BF16) for m in tables]
        + [
            pltpu.VMEM((9, e, NODES), F32),
            pltpu.VMEM((9 * e, NODES), BF16),
            pltpu.VMEM((9 * e, NODES), BF16),
            pltpu.VMEM((9, e, NODES), F32),
            pltpu.VMEM((2 * faces, 6 * FACE), BF16),
            pltpu.VMEM((2, 2 * pair, 6 * FACE), BF16),
            pltpu.VMEM((faces, 2 * faces), BF16),
            pltpu.VMEM((4 * e, 2 * pair), BF16),
            pltpu.VMEM((2 * pair, 4 * e), BF16),
            pltpu.VMEM((4, 4, cap, 6 * FACE), F32),
            pltpu.VMEM((4, 4, cap, 6 * FACE), F32),
            pltpu.VMEM((2, cap, 8 * FACE), F32),
            pltpu.VMEM((2, cap, 8 * FACE), F32),
            pltpu.VMEM((2 * e, 6 * FACE), F32),
            pltpu.VMEM((2 * e, 6 * FACE), F32),
            pltpu.VMEM((pair, 6 * FACE), F32),
            pltpu.VMEM((pair, 4 * e), BF16),
            pltpu.VMEM((GROUPS, n_seg, chunk, 9 // GROUPS * 128), F32),
            pltpu.VMEM((GROUPS, n_seg, chunk, 9 // GROUPS * 128), F32),
            dma((5,)),
            dma((7,)),
            dma((4, 4)),
            dma((4, 4)),
            dma((2,)),
            dma((2,)),
            dma((GROUPS, n_seg - 1)),
            dma((GROUPS, n_seg - 1)),
        ],
        compiler_params=pltpu.CompilerParams(
            collective_id=0, has_side_effects=True, vmem_limit_bytes=60 * 2**20
        ),
    )(material, send_faces, face_partner.T, migration, children, adjoint, *tables)
    return pl.pallas_call(
        hand_over,
        out_shape=shapes,
        in_specs=[vmem, vmem],
        out_specs=(away, away),
        scratch_shapes=[dma((2,))],
    )(*(pltpu.with_memory_space_constraint(x, pltpu.VMEM) for x in results))


def solution(mesh):
    both = ("curve", "seg")
    in_specs = (
        P(None, both, None),
        P(None, both),
        P(both, None),
        P(both, None, None),
        P(None, both),
        P(None, both),
    )
    out_specs = (P(None, both, None), P(None, both, None))
    body = functools.partial(shards, mesh.shape["curve"], mesh.shape["seg"])
    return jax.shard_map(
        body, mesh=mesh, in_specs=in_specs, out_specs=out_specs, check_vma=False
    )
```

```python
import functools

import jax
import jax.numpy as jnp
import numpy as np
from jax import lax
from jax.experimental import pallas as pl
from jax.experimental.pallas import tpu as pltpu
from jax.sharding import PartitionSpec as P

V = ((3, 8, 7), (8, 4, 6), (7, 6, 5))
F32 = jnp.float32
BF16 = jnp.bfloat16
NP = 8
NODES = NP**3
FACE = NP**2
HALF = NODES // 2
STEP = 0.8 / NP**2
GAIN = 0.5 * 0.5 * NP * (NP - 1)
SLOTS = 2
GROUPS = 1


def lobatto_nodes():
    return -np.cos(np.pi * np.arange(NP) / (NP - 1))


def derivative_line():
    points = lobatto_nodes()
    ids = np.arange(NP)
    weight = np.where((ids == 0) | (ids == NP - 1), 2.0, 1.0)
    row, col = ids[:, None], ids[None, :]
    gap = np.where(row == col, 1.0, points[:, None] - points[None, :])
    matrix = weight[:, None] / weight[None, :] * (-1.0) ** (row + col) / gap
    matrix = np.where(row == col, 0.0, matrix)
    return matrix - np.eye(NP) * matrix.sum(axis=1)[:, None]


def refine_line(upper):
    points = lobatto_nodes()
    targets = (points + (2.0 * upper - 1.0)) / 2.0
    columns = []
    for column in range(NP):
        factor = np.ones(NP)
        for other in range(NP):
            if other != column:
                factor = factor * (targets - points[other]) / (points[column] - points[other])
        columns.append(factor)
    return np.stack(columns, axis=1)


def two_parts(matrix):
    matrix = np.asarray(matrix, np.float32)
    high = matrix.astype(jnp.bfloat16)
    low = (matrix - high.astype(np.float32)).astype(jnp.bfloat16)
    return high, low


def three_deep(matrix):
    high, low = two_parts(matrix)
    return np.concatenate([high, high, low], axis=0)


def line_operators(line):
    return (
        np.kron(line, np.eye(FACE)),
        np.kron(np.kron(np.eye(4), line), np.eye(NP)),
        np.kron(np.eye(32), line),
    )


def constants():
    line = derivative_line()
    line[0, 0] += GAIN
    line[NP - 1, NP - 1] -= GAIN
    derivs = [three_deep(m) for m in line_operators(line)]
    halves = [line_operators(refine_line(b)) for b in range(2)]
    quads = [
        halves[k // 2][1] @ halves[k % 2][2] for k in range(4)
    ]
    refines = [
        three_deep(np.concatenate([halves[0][0], halves[1][0]], axis=0)),
        three_deep(np.concatenate(quads, axis=0)),
    ]
    ids = np.arange(NODES).reshape(NP, NP, NP)
    spreads = []
    for d in (1, 2):
        spread = np.zeros((2, FACE, NODES))
        for s in range(2):
            nodes = np.take(ids, 0 if s == 0 else NP - 1, axis=d).reshape(-1)
            spread[s, np.arange(FACE), nodes] = GAIN if s == 0 else -GAIN
        spread = spread.reshape(2 * FACE, NODES).astype(jnp.bfloat16)
        spreads.append(np.concatenate([spread, spread], axis=0))
    return derivs + refines + spreads


def split(x):
    high = x.astype(BF16)
    return high, (x - high.astype(F32)).astype(BF16)


def dot(a, b):
    return jnp.dot(a, b, preferred_element_type=F32)


def iota(shape, dim):
    return lax.broadcasted_iota(jnp.int32, shape, dim)


def column(row, count):
    n = row.shape[1]
    hit = iota((count, n), 0) % n == iota((count, n), 1)
    return jnp.sum(jnp.where(hit, jnp.broadcast_to(row, (count, n)), 0.0), axis=1, keepdims=True)


def kernel(
    n_curve, n_seg, e, cap, parents,
    *refs
):
    given, hbm, refs = refs[:5], refs[5:13], refs[13:]
    (
        out, par,
        mat, partner, send, mig, child,
        adj, d0, d1, d2, r0, r1, spread_y, spread,
        w, xh, xl, vol, table, far_table, pick, far_pick, sendpick,
        outbox, inbox, tie_out, tie_in, held, coef, coef0, late, echo, pay, arrived,
        small_sem, load_sem, send_sem, recv_sem, tie_send, tie_recv, mig_send, mig_recv,
    ) = refs
    homes = (adj, d0, d1, d2, r0, r1, spread_y, spread)
    loads = [
        pltpu.make_async_copy(hbm[k], homes[k], load_sem.at[k]) for k in range(len(homes))
    ]
    loads.append(pltpu.make_async_copy(hbm[0], w, load_sem.at[8]))
    early = (8, 0, 1, 2, 3, 6, 7)
    small = [
        pltpu.make_async_copy(a, b, small_sem.at[k])
        for k, (a, b) in enumerate(zip(given, (mat, send, partner, mig, child)))
    ]
    for copy in small[:2]:
        copy.start()
    loads[early[0]].start()
    for copy in small[2:]:
        copy.start()
    for k in early[1:] + (5, 4):
        loads[k].start()
    ci = lax.axis_index("curve")
    si = lax.axis_index("seg")
    cm = lax.rem(ci + n_curve - 1, n_curve)
    cp = lax.rem(ci + 1, n_curve)
    sm = lax.rem(si + n_seg - 1, n_seg)
    sp = lax.rem(si + 1, n_seg)
    sides = ((cm, si), (cp, si), (ci, sm), (ci, sp))
    barrier = pltpu.get_barrier_semaphore()
    MESH = pl.DeviceIdType.MESH
    for c in (cm, cp):
        pl.semaphore_signal(barrier, inc=1, device_id=(c, si), device_id_type=MESH)
    for k in range(1, n_seg):
        pl.semaphore_signal(
            barrier, inc=1, device_id=(ci, lax.rem(si + k, n_seg)), device_id_type=MESH
        )


    faces = 6 * e
    pair = 2 * cap
    small[1].wait()
    derivs = (d0, d1, d2)

    def codes(rows):
        k = iota((rows, faces), 1)
        return (6 * (k % e) + k // e).astype(F32)

    for r in range(4):
        k = iota((cap, 2 * e), 1)
        code = (6 * (k % e) + k // e + 2 * (r // 2)).astype(F32)
        want = column(send[0, r : r + 1, :].astype(F32), cap)
        hit = jnp.where(code == want, 1.0, 0.0).astype(BF16)
        sendpick[r * cap : (r + 1) * cap, :] = jnp.concatenate([hit, hit], axis=1)

    small[0].wait()
    density = jnp.broadcast_to(1.0 / column(mat[0:1, :], e), (e, NODES))
    lame = jnp.broadcast_to(column(mat[1:2, :], e), (e, NODES))
    shear = jnp.broadcast_to(column(mat[2:3, :], e), (e, NODES))

    loads[early[0]].wait()
    low_half = iota((e, 2 * FACE), 1) < FACE

    def comps(d):
        return [V[d][0] - 3, V[d][1] - 3, V[d][2] - 3, 6, 7, 8]

    def rows(d):
        return [0, 1, 2, V[0][d], V[1][d], V[2][d]]

    lane = iota((e, 2 * FACE), 1)
    spot = lane % FACE
    group = spot // (2 * NP)

    def paths(d):
        stride = (None, 1, NP)[d]
        start = spot % (2 * NP) // NP * FACE + spot % NP * stride
        reach = FACE - NP if d == 1 else NP - 1
        return start + jnp.where(low_half, 0, reach)

    def gather(v, path):
        return jnp.take_along_axis(v, path, axis=1, mode="promise_in_bounds")

    def trace_pair(a, b, d):
        picks = []
        path = paths(d)
        for v in (a, b):
            got = gather(v[:, : 2 * FACE], path)
            for j in range(1, 4):
                part = gather(v[:, j * 2 * FACE : (j + 1) * 2 * FACE], path)
                got = jnp.where(group == j, part, got)
            picks.append(got)
        a, b = picks
        return (
            jnp.where(low_half, a, pltpu.roll(b, FACE, 1)),
            jnp.where(low_half, pltpu.roll(a, FACE, 1), b),
        )

    def lift_paths(d):
        along = lane % FACE // NP if d == 1 else lane % NP
        across = lane % NP if d == 1 else lane % FACE // NP
        back = lane // FACE * NP + across
        gain = jnp.where(along == 0, GAIN, jnp.where(along == NP - 1, -GAIN, 0.0))
        starts = [
            jnp.where(along == NP - 1, FACE, 0) + j * 2 * NP + back for j in range(4)
        ]
        return starts, gain.astype(F32)

    def lift(v, d):
        starts, gain = lift_paths(d)
        return jnp.concatenate([gather(v, path) * gain for path in starts], axis=1)

    def face_copy(step, r):
        return pltpu.make_async_remote_copy(
            src_ref=outbox.at[step, r],
            dst_ref=inbox.at[step, r ^ 1],
            send_sem=send_sem.at[step, r],
            recv_sem=recv_sem.at[step, r ^ 1],
            device_id=sides[r],
            device_id_type=MESH,
        )

    def tie_copy(r):
        return pltpu.make_async_remote_copy(
            src_ref=tie_out.at[r - 2],
            dst_ref=tie_in.at[(r ^ 1) - 2],
            send_sem=tie_send.at[r - 2],
            recv_sem=tie_recv.at[(r ^ 1) - 2],
            device_id=sides[r],
            device_id_type=MESH,
        )

    def send_side(step, d, source):
        picked = dot(sendpick[d * pair : (d + 1) * pair, :], source)
        outbox[step, 2 * d : 2 * d + 2] = picked.reshape(2, cap, 6 * FACE)
        for r in (2 * d, 2 * d + 1):
            face_copy(step, r).start()

    def y_faces():
        trace = lame * (w[3] + w[4] + w[5])
        images = [shear * w[V[1][k]] for k in range(3)]
        images[1] = 2.0 * images[1] + trace
        images += [density * w[k] for k in range(3)]
        pairs = [trace_pair(images[2 * p], images[2 * p + 1], 1) for p in range(3)]
        return jnp.concatenate(
            [jnp.concatenate([p[s] for p in pairs], axis=1) for s in range(2)], axis=0
        )

    def x_faces():
        sides2 = []
        for s, cols in ((0, slice(0, 2 * FACE)), (1, slice(NODES - 2 * FACE, NODES))):
            rho, lam, mu = narrow
            trace = lam * (w[3, :, cols] + w[4, :, cols] + w[5, :, cols])
            images = [mu * w[V[0][k], :, cols] for k in range(3)]
            images[0] = 2.0 * images[0] + trace
            images += [rho * w[k, :, cols] for k in range(3)]
            values = []
            for p in range(3):
                a, b = images[2 * p], images[2 * p + 1]
                if s == 0:
                    values.append(jnp.where(low_half, a, pltpu.roll(b, FACE, 1)))
                else:
                    values.append(jnp.where(low_half, pltpu.roll(a, FACE, 1), b))
            sides2.append(jnp.concatenate(values, axis=1))
        return jnp.concatenate(sides2, axis=0)

    def send_y(step, both):
        send_side(step, 1, jnp.concatenate(split(both), axis=0))
        held[...] = both

    def send_x(step, both):
        high, low = split(both)
        table[: 2 * e, :] = high
        table[4 * e : 6 * e, :] = low
        send_side(step, 0, jnp.concatenate([high, low], axis=0))

    def edges(blocks, d):
        line, across = spot // NP, spot % NP
        path = jnp.where(line == NP - 1, FACE, 0) + jnp.where(low_half, 0, FACE - NP) + across
        gain = jnp.where(line == 0, GAIN, jnp.where(line == NP - 1, -GAIN, 0.0)).astype(F32)
        rho, lam, mu = (v * gain for v in narrow)
        u = [rho * gather(blocks[k], path) for k in range(3)]
        a, b = gather(blocks[3], path), gather(blocks[4], path)
        images = [lam * b, mu * a] if d == 0 else [mu * b, lam * a]
        return images + [None] + u

    def paired(images):
        sides2 = [[], []]
        for p in range(3):
            a, b = images[2 * p], images[2 * p + 1]
            if a is None:
                sides2[0].append(jnp.where(low_half, 0.0, pltpu.roll(b, FACE, 1)))
                sides2[1].append(jnp.where(low_half, 0.0, b))
            else:
                sides2[0].append(jnp.where(low_half, a, pltpu.roll(b, FACE, 1)))
                sides2[1].append(jnp.where(low_half, pltpu.roll(a, FACE, 1), b))
        return jnp.concatenate([jnp.concatenate(v, axis=1) for v in sides2], axis=0)

    def swap(v):
        n = v.shape[0]
        low = iota((n, 2 * FACE), 1) < FACE
        r = [pltpu.roll(v[:, k * 2 * FACE : (k + 1) * 2 * FACE], FACE, 1) for k in range(3)]
        return jnp.concatenate(
            [jnp.where(low, r[(k + 1) % 3], r[(k + 2) % 3]) for k in range(3)], axis=1
        )

    def onto_first(first, last):
        first, last = first * GAIN, last * -GAIN
        pieces = []
        for c in range(6):
            p, odd = c // 2, c % 2
            a = first[:, p * 2 * FACE : (p + 1) * 2 * FACE]
            b = last[:, p * 2 * FACE : (p + 1) * 2 * FACE]
            if odd:
                a = pltpu.roll(a, FACE, 1)
            else:
                b = pltpu.roll(b, FACE, 1)
            pieces.append((jnp.where(low_half, a, 0.0), jnp.where(low_half, 0.0, b)))
        return pieces

    def face_rows(lower, upper):
        blocks = []
        for c in range(6):
            p, odd = c // 2, c % 2
            a = lower[:, p * 2 * FACE : (p + 1) * 2 * FACE]
            b = upper[:, p * 2 * FACE : (p + 1) * 2 * FACE]
            if odd:
                a = pltpu.roll(a, FACE, 1)
            else:
                b = pltpu.roll(b, FACE, 1)
            blocks.append(jnp.where(low_half, a, b))
        return blocks

    narrow = [v[:, : 2 * FACE] for v in (density, lame, shear)]
    scale = jnp.concatenate(
        [
            jnp.where(low_half, narrow[2], 2.0 * narrow[2] + narrow[1]),
            jnp.where(low_half, narrow[2], narrow[0]),
            narrow[0],
        ],
        axis=1,
    )
    scale0 = jnp.concatenate(
        [
            jnp.where(low_half, 2.0 * narrow[2] + narrow[1], narrow[2]),
            jnp.where(low_half, narrow[2], narrow[0]),
            narrow[0],
        ],
        axis=1,
    )
    first = y_faces(), x_faces()
    pl.semaphore_wait(barrier, 1 + n_seg)
    send_y(0, first[0])
    send_x(0, first[1])
    code = codes(e)
    wants = []
    for copy in small[2:]:
        copy.wait()
    for f in range(6):
        want = column(partner[f : f + 1, :].astype(F32), e)
        wants.append(want)
        hit = jnp.where(code == want, 1.0, 0.0).astype(BF16)
        outer, inner = hit[:, : 4 * e], hit[:, 4 * e :]
        pick[f * e : (f + 1) * e, :] = jnp.concatenate([outer, outer, inner, inner], axis=1)
        if f < 4:
            slot_code = (iota((e, pair), 1) + faces + (f // 2) * pair).astype(F32)
            far = jnp.where(slot_code == want, 1.0, 0.0).astype(BF16)
            far_pick[f * e : (f + 1) * e, :] = jnp.concatenate([far, far], axis=1)
    coef0[:e, :] = GAIN * scale0
    coef0[e:, :] = -GAIN * scale0
    coef[:e, :] = GAIN * scale
    coef[e:, :] = -GAIN * scale
    ties = jnp.concatenate(
        [
            jnp.concatenate([GAIN * scale, jnp.broadcast_to(wants[2], (e, 2 * FACE))], axis=1),
            jnp.concatenate([-GAIN * scale, jnp.broadcast_to(wants[3], (e, 2 * FACE))], axis=1),
        ],
        axis=0,
    )
    picked = dot(sendpick[pair:, :], jnp.concatenate(split(ties), axis=0))
    tie_out[...] = picked.reshape(2, cap, 8 * FACE)
    for r in (2, 3):
        tie_copy(r).start()
    late[...] = jnp.zeros_like(late)
    own = si.astype(F32)
    kids = mig[...].astype(F32)
    owner, slot, octant = kids[0:1, :], kids[1:2, :], kids[2:3, :]
    key = jnp.where(owner == own, slot, parents + owner * SLOTS + slot)
    key_col = column(key, e)
    earlier = jnp.where(key_col < jnp.broadcast_to(key, (e, e)), 1.0, 0.0)
    rank = jnp.sum(earlier, axis=0, keepdims=True) * 0.125
    rank_col = column(rank, e)
    place = octant * parents + rank
    perm = jnp.where(iota((e, e), 0).astype(F32) == jnp.broadcast_to(place, (e, e)), 1.0, 0.0)
    perm = perm.astype(BF16)
    perm = jnp.concatenate([perm, perm], axis=1)
    per = 9 // GROUPS
    tiles = NODES // 128
    wide = 2 * tiles * parents
    strip = iota((e, wide), 1)
    member = rank_col == (strip % parents).astype(F32)
    group_key = jnp.sum(jnp.where(member, key_col, 0.0), axis=0, keepdims=True) * 0.125
    chunk = SLOTS * tiles
    total_rows = n_seg * chunk
    row = iota((total_rows, wide), 0)
    col = iota((total_rows, wide), 1)
    wanted = (parents + row // tiles).astype(F32)
    match = jnp.where(wanted == jnp.broadcast_to(group_key, (total_rows, wide)), 1.0, 0.0)
    same = (row % tiles) == (col // parents) % tiles
    chooser = jnp.where(same, match, 0.0).astype(BF16)
    nrow = tiles * parents
    family = child[...].astype(F32)
    holder = column(family[0:1, :], nrow)
    fslot = jnp.maximum(column(family[1:2, :], nrow), 0.0)
    at_home = holder == own
    r = iota((nrow, wide), 0)
    c = iota((nrow, wide), 1)
    home = (r % parents).astype(F32) == jnp.broadcast_to(group_key, (nrow, wide))
    home = jnp.where(home, 1.0, 0.0) * jnp.where(at_home, 1.0, 0.0)
    home = jnp.where(r // parents == (c // parents) % tiles, home, 0.0).astype(BF16)
    r = iota((nrow, total_rows), 0)
    c = iota((nrow, total_rows), 1)
    source = (holder * SLOTS + fslot) == (c // tiles).astype(F32)
    away = jnp.where(source, 1.0, 0.0) * jnp.where(at_home, 0.0, 1.0)
    away = jnp.where(r // parents == c % tiles, away, 0.0).astype(BF16)
    for g in range(GROUPS):
        arrived[g, pl.ds(si, 1)] = jnp.zeros((1, chunk, per * 128), F32)
    for k in early[1:]:
        loads[k].wait()

    def three(picks, cols=slice(0, NODES)):
        high = jnp.concatenate([xh[c * e : (c + 1) * e, cols] for c in picks], axis=0)
        low = jnp.concatenate([xl[c * e : (c + 1) * e, cols] for c in picks], axis=0)
        return jnp.concatenate([high, low, high], axis=1)

    def stage(step, carry):
        trace = lame * (w[3] + w[4] + w[5])
        fields = [2.0 * (shear * w[3 + k]) + trace for k in range(3)]
        fields += [shear * w[6 + k] for k in range(3)]
        fields += [density * w[k] for k in range(3)]
        high, low = split(held[...])
        table[2 * e : 4 * e, :] = high
        table[6 * e : 8 * e, :] = low
        near = dot(pick[:, : 8 * e], table[: 8 * e, :])
        for k in range(9):
            high, low = split(fields[k])
            xh[k * e : (k + 1) * e, :] = high
            xl[k * e : (k + 1) * e, :] = low

        part0 = dot(three(comps(0)), d0[...])
        keep = jnp.where(step == 0, -4.0 / 3.0, jnp.where(step == 2, 2.0 / 3.0, 1.0 / 3.0))
        keep = keep.astype(F32)
        for k in range(9):
            out[k] = jnp.where(step == 0, 0.0, out[k]) + keep * w[k]

        cd = comps(2)
        for p in range(3):
            cols = slice(p * 2 * FACE, (p + 1) * 2 * FACE)
            pair2 = trace_pair(fields[cd[2 * p]], fields[cd[2 * p + 1]], 2)
            for s, value in enumerate(pair2):
                high, low = split(value)
                table[(8 + s) * e : (9 + s) * e, cols] = high
                table[(10 + s) * e : (11 + s) * e, cols] = low
        near = near + dot(pick[:, 8 * e :], table[8 * e :, :])
        side = [near[f * e : (f + 1) * e, :] for f in range(6)]
        ahead = jnp.where(step < 2, 0.5 * STEP, jnp.where(step == 2, STEP, STEP / 6.0))
        ahead = ahead.astype(F32)
        seen = set()
        for d in range(3):
            if d == 0:
                parts = [part0]
            else:
                sides2 = face_rows(side[2 * d], side[2 * d + 1])
                if d == 1:
                    lifts = [lift(v, d) for v in sides2]
                    parts = [
                        dot(three(comps(d), slice(h * HALF, (h + 1) * HALF)), derivs[d][...])
                        for h in range(2)
                    ]
                else:
                    edge = jnp.concatenate(split(jnp.concatenate(sides2, axis=0)), axis=1)
                    parts = [
                        dot(
                            jnp.concatenate(
                                [three(comps(d), slice(h * HALF, (h + 1) * HALF)), edge], axis=1
                            ),
                            jnp.concatenate(
                                [derivs[d][...], spread[:, h * HALF : (h + 1) * HALF]], axis=0
                            ),
                        )
                        for h in range(2)
                    ]
            width = NODES // len(parts)
            for c, row in enumerate(rows(d)):
                for h, part in enumerate(parts):
                    piece = part[c * e : (c + 1) * e, :]
                    cols = slice(h * width, (h + 1) * width)
                    if d == 1:
                        piece = piece + lifts[c][:, cols]
                    if row in seen:
                        vol[row, :, cols] += piece
                    else:
                        vol[row, :, cols] = piece
                seen.add(row)
        for row, (a, b) in zip(rows(0), onto_first(side[0], side[1])):
            vol[row, :, : 2 * FACE] += a
            vol[row, :, -2 * FACE :] += b
        for k in range(9):
            w[k] = adj[k] + ahead * vol[k]

        def far(d, got):
            high, low = split(got)
            far_table[d, :pair, :] = high
            far_table[d, pair:, :] = low
            return dot(far_pick[2 * d * e : 2 * (d + 1) * e, :], far_table[d])

        def arrive(d):
            for r in (2 * d, 2 * d + 1):
                face_copy(step, r).wait()
            got = inbox[step, 2 * d : 2 * d + 2].reshape(pair, 6 * FACE)
            if d == 1:
                got = got + late[...]
            picked = far(d, got)
            return picked, face_rows(picked[:e], picked[e:])

        def apply_x(picked):
            for row, (a, b) in zip(rows(0), onto_first(picked[:e], picked[e:])):
                w[row, :, : 2 * FACE] += ahead * a
                w[row, :, -2 * FACE :] += ahead * b

        def apply_y(blocks):
            edge = jnp.concatenate(split(jnp.concatenate(blocks, axis=0)), axis=1)
            lifted = dot(edge, spread_y[...])
            for c, row in enumerate(rows(1)):
                w[row] += ahead * lifted[c * e : (c + 1) * e, :]

        @pl.when(step < 3)
        def _():
            base = y_faces()
            base_x = x_faces()
            picked, blocks = arrive(0)
            send_y(step + 1, base + ahead * paired(edges(blocks, 1)))
            base_x = base_x + ahead * (coef0[...] * swap(picked))
            apply_x(picked)
            picked, blocks = arrive(1)
            source = jnp.concatenate(
                [table[2 * e : 4 * e, :], table[6 * e : 8 * e, :]], axis=0
            )
            send_x(step + 1, base_x + ahead * paired(edges(blocks, 0)))
            apply_y(blocks)
            held[...] = held[...] + ahead * (coef[...] * swap(picked))

            @pl.when(step == 0)
            def _():
                for r in (2, 3):
                    tie_copy(r).wait()
                told = tie_in[:, :, 6 * FACE :].reshape(pair, 2 * FACE)[:, :pair]
                slot = iota((pair, pair), 1)
                mine = faces + (3 - slot // cap) * cap + slot % cap
                link = jnp.where(told == mine.astype(F32), 1.0, 0.0).astype(BF16)
                echo[...] = dot(link, sendpick[pair:, :]).astype(BF16)

            ours = dot(echo[...], source)
            late[...] = ahead * (tie_in[:, :, : 6 * FACE].reshape(pair, 6 * FACE) * swap(ours))

        @pl.when(step == 3)
        def _():
            apply_x(arrive(0)[0])
            apply_y(arrive(1)[1])

        return carry

    lax.fori_loop(0, 4, stage, 0)
    for k in (4, 5):
        loads[k].wait()

    def fold(values, matrix, ways, blocks):
        count = len(values)
        groups = [[] for _ in range(ways)]
        for v in values:
            octants = v.shape[0] // parents
            for way in range(ways):
                for c in range(way, octants, ways):
                    groups[way].append(v[c * parents : (c + 1) * parents, :])
        sides2 = [split(jnp.concatenate(p, axis=0)) for p in groups]
        width = NODES // blocks
        results = []
        for h in range(blocks):
            cols = slice(h * width, (h + 1) * width)
            high = jnp.concatenate([s[0][:, cols] for s in sides2], axis=1)
            low = jnp.concatenate([s[1][:, cols] for s in sides2], axis=1)
            results.append(dot(jnp.concatenate([high, low, high], axis=1), matrix[...]))
        total = results[0] if blocks == 1 else jnp.concatenate(results, axis=1)
        m = total.shape[0] // count
        return [total[k * m : (k + 1) * m, :] for k in range(count)]

    def migration_copy(g, k):
        to = lax.rem(si + k, n_seg)
        return pltpu.make_async_remote_copy(
            src_ref=pay.at[g, to],
            dst_ref=arrived.at[g, si],
            send_sem=mig_send.at[g, k - 1],
            recv_sem=mig_recv.at[g, k - 1],
            device_id=(ci, to),
            device_id_type=MESH,
        )

    local = []
    for g in range(GROUPS):
        ordered = []
        for k in range(g * per, (g + 1) * per):
            total = out[k] + w[k]
            out[k] = total
            ordered.append(dot(perm, jnp.concatenate(split(total), axis=0)))
        sums = fold(fold(ordered, r1, 4, 2), r0, 2, 1)
        stacked = jnp.concatenate(
            [
                jnp.concatenate([s[:, k * 128 : (k + 1) * 128] for s in sums], axis=1)
                for k in range(tiles)
            ],
            axis=0,
        )
        both = jnp.concatenate(split(stacked), axis=0)
        pay[g] = dot(chooser, both).reshape(n_seg, chunk, per * 128)
        for k in range(1, n_seg):
            migration_copy(g, k).start()
        local.append(dot(home, both))
    for g in range(GROUPS):
        for k in range(1, n_seg):
            migration_copy(g, k).wait()
        ah, al = split(arrived[g].reshape(total_rows, per * 128))
        result = local[g] + dot(
            jnp.concatenate([away, away], axis=1), jnp.concatenate([ah, al], axis=0)
        )
        for k in range(per):
            for t in range(tiles):
                par[g * per + k, :, t * 128 : (t + 1) * 128] = result[
                    t * parents : (t + 1) * parents, k * 128 : (k + 1) * 128
                ]


def hand_over(a_in, b_in, a_out, b_out, sems):
    copies = [
        pltpu.make_async_copy(a_in, a_out, sems.at[0]),
        pltpu.make_async_copy(b_in, b_out, sems.at[1]),
    ]
    for copy in copies:
        copy.start()
    for copy in copies:
        copy.wait()


def shards(n_curve, n_seg, adjoint, material, face_partner, send_faces, migration, children):
    e = adjoint.shape[1]
    cap = send_faces.shape[2]
    parents = children.shape[1]
    tables = [jnp.asarray(m) for m in constants()]
    faces, pair = 6 * e, 2 * cap
    chunk = SLOTS * (NODES // 128)
    vmem = pl.BlockSpec(memory_space=pltpu.VMEM)
    away = pl.BlockSpec(memory_space=pl.ANY)
    dma = pltpu.SemaphoreType.DMA
    shapes = (
        jax.ShapeDtypeStruct((9, e, NODES), F32),
        jax.ShapeDtypeStruct((9, parents, NODES), F32),
    )
    results = pl.pallas_call(
        functools.partial(kernel, n_curve, n_seg, e, cap, parents),
        out_shape=tuple(pltpu.VMEM(x.shape, F32) for x in shapes),
        in_specs=[away] * (6 + len(tables)),
        out_specs=(vmem, vmem),
        scratch_shapes=[
            pltpu.VMEM((3, e), F32),
            pltpu.VMEM((6, e), jnp.int32),
            pltpu.VMEM(send_faces.shape, jnp.int32),
            pltpu.VMEM((3, e), jnp.int32),
            pltpu.VMEM((2, parents), jnp.int32),
            pltpu.VMEM((9, e, NODES), F32),
        ]
        + [pltpu.VMEM(m.shape, BF16) for m in tables]
        + [
            pltpu.VMEM((9, e, NODES), F32),
            pltpu.VMEM((9 * e, NODES), BF16),
            pltpu.VMEM((9 * e, NODES), BF16),
            pltpu.VMEM((9, e, NODES), F32),
            pltpu.VMEM((2 * faces, 6 * FACE), BF16),
            pltpu.VMEM((2, 2 * pair, 6 * FACE), BF16),
            pltpu.VMEM((faces, 2 * faces), BF16),
            pltpu.VMEM((4 * e, 2 * pair), BF16),
            pltpu.VMEM((2 * pair, 4 * e), BF16),
            pltpu.VMEM((4, 4, cap, 6 * FACE), F32),
            pltpu.VMEM((4, 4, cap, 6 * FACE), F32),
            pltpu.VMEM((2, cap, 8 * FACE), F32),
            pltpu.VMEM((2, cap, 8 * FACE), F32),
            pltpu.VMEM((2 * e, 6 * FACE), F32),
            pltpu.VMEM((2 * e, 6 * FACE), F32),
            pltpu.VMEM((2 * e, 6 * FACE), F32),
            pltpu.VMEM((pair, 6 * FACE), F32),
            pltpu.VMEM((pair, 4 * e), BF16),
            pltpu.VMEM((GROUPS, n_seg, chunk, 9 // GROUPS * 128), F32),
            pltpu.VMEM((GROUPS, n_seg, chunk, 9 // GROUPS * 128), F32),
            dma((5,)),
            dma((9,)),
            dma((4, 4)),
            dma((4, 4)),
            dma((2,)),
            dma((2,)),
            dma((GROUPS, n_seg - 1)),
            dma((GROUPS, n_seg - 1)),
        ],
        compiler_params=pltpu.CompilerParams(
            collective_id=0, has_side_effects=True, vmem_limit_bytes=60 * 2**20
        ),
    )(material, send_faces, face_partner.T, migration, children, adjoint, *tables)
    return pl.pallas_call(
        hand_over,
        out_shape=shapes,
        in_specs=[vmem, vmem],
        out_specs=(away, away),
        scratch_shapes=[dma((2,))],
    )(*(pltpu.with_memory_space_constraint(x, pltpu.VMEM) for x in results))


def solution(mesh):
    both = ("curve", "seg")
    in_specs = (
        P(None, both, None),
        P(None, both),
        P(both, None),
        P(both, None, None),
        P(None, both),
        P(None, both),
    )
    out_specs = (P(None, both, None), P(None, both, None))
    body = functools.partial(shards, mesh.shape["curve"], mesh.shape["seg"])
    return jax.shard_map(
        body, mesh=mesh, in_specs=in_specs, out_specs=out_specs, check_vma=False
    )
```

```python
import functools

import jax
import jax.numpy as jnp
import numpy as np
from jax import lax
from jax.experimental import pallas as pl
from jax.experimental.pallas import tpu as pltpu
from jax.sharding import PartitionSpec as P

V = ((3, 8, 7), (8, 4, 6), (7, 6, 5))
F32 = jnp.float32
BF16 = jnp.bfloat16
NP = 8
NODES = NP**3
FACE = NP**2
HALF = NODES // 2
STEP = 0.8 / NP**2
GAIN = 0.5 * 0.5 * NP * (NP - 1)
SLOTS = 2
GROUPS = 1


def lobatto_nodes():
    return -np.cos(np.pi * np.arange(NP) / (NP - 1))


def derivative_line():
    points = lobatto_nodes()
    ids = np.arange(NP)
    weight = np.where((ids == 0) | (ids == NP - 1), 2.0, 1.0)
    row, col = ids[:, None], ids[None, :]
    gap = np.where(row == col, 1.0, points[:, None] - points[None, :])
    matrix = weight[:, None] / weight[None, :] * (-1.0) ** (row + col) / gap
    matrix = np.where(row == col, 0.0, matrix)
    return matrix - np.eye(NP) * matrix.sum(axis=1)[:, None]


def refine_line(upper):
    points = lobatto_nodes()
    targets = (points + (2.0 * upper - 1.0)) / 2.0
    columns = []
    for column in range(NP):
        factor = np.ones(NP)
        for other in range(NP):
            if other != column:
                factor = factor * (targets - points[other]) / (points[column] - points[other])
        columns.append(factor)
    return np.stack(columns, axis=1)


def two_parts(matrix):
    matrix = np.asarray(matrix, np.float32)
    high = matrix.astype(jnp.bfloat16)
    low = (matrix - high.astype(np.float32)).astype(jnp.bfloat16)
    return high, low


def three_deep(matrix):
    high, low = two_parts(matrix)
    return np.concatenate([high, high, low], axis=0)


def line_operators(line):
    return (
        np.kron(line, np.eye(FACE)),
        np.kron(np.kron(np.eye(4), line), np.eye(NP)),
        np.kron(np.eye(32), line),
    )


def constants():
    line = derivative_line()
    line[0, 0] += GAIN
    line[NP - 1, NP - 1] -= GAIN
    derivs = [three_deep(m) for m in line_operators(line)]
    halves = [line_operators(refine_line(b)) for b in range(2)]
    quads = [
        halves[k // 2][1] @ halves[k % 2][2] for k in range(4)
    ]
    refines = [
        three_deep(np.concatenate([halves[0][0], halves[1][0]], axis=0)),
        three_deep(np.concatenate(quads, axis=0)),
    ]
    ids = np.arange(NODES).reshape(NP, NP, NP)
    spreads = []
    for d in (1, 2):
        spread = np.zeros((2, FACE, NODES))
        for s in range(2):
            nodes = np.take(ids, 0 if s == 0 else NP - 1, axis=d).reshape(-1)
            spread[s, np.arange(FACE), nodes] = GAIN if s == 0 else -GAIN
        spread = spread.reshape(2 * FACE, NODES).astype(jnp.bfloat16)
        spreads.append(np.concatenate([spread, spread], axis=0))
    return derivs + refines + spreads


def split(x):
    high = x.astype(BF16)
    return high, (x - high.astype(F32)).astype(BF16)


def dot(a, b):
    return jnp.dot(a, b, preferred_element_type=F32)


def iota(shape, dim):
    return lax.broadcasted_iota(jnp.int32, shape, dim)


def column(row, count):
    n = row.shape[1]
    hit = iota((count, n), 0) % n == iota((count, n), 1)
    return jnp.sum(jnp.where(hit, jnp.broadcast_to(row, (count, n)), 0.0), axis=1, keepdims=True)


def kernel(
    n_curve, n_seg, e, cap, parents,
    *refs
):
    given, hbm, refs = refs[:5], refs[5:13], refs[13:]
    (
        out, par,
        mat, partner, send, mig, child,
        adj, d0, d1, d2, r0, r1, spread_y, spread,
        w, xh, xl, vol, table, far_table, pick, far_pick, sendpick,
        outbox, inbox, tie_out, tie_in, held, coef, coef0, late, echo, pay, arrived,
        small_sem, load_sem, send_sem, recv_sem, tie_send, tie_recv, mig_send, mig_recv,
    ) = refs
    homes = (adj, d0, d1, d2, r0, r1, spread_y, spread)
    loads = [
        pltpu.make_async_copy(hbm[k], homes[k], load_sem.at[k]) for k in range(len(homes))
    ]
    loads.append(pltpu.make_async_copy(hbm[0], w, load_sem.at[8]))
    early = (8, 0, 1, 2, 3, 6, 7)
    small = [
        pltpu.make_async_copy(a, b, small_sem.at[k])
        for k, (a, b) in enumerate(zip(given, (mat, send, partner, mig, child)))
    ]
    for copy in small[:2]:
        copy.start()
    loads[early[0]].start()
    for copy in small[2:]:
        copy.start()
    ci = lax.axis_index("curve")
    si = lax.axis_index("seg")
    cm = lax.rem(ci + n_curve - 1, n_curve)
    cp = lax.rem(ci + 1, n_curve)
    sm = lax.rem(si + n_seg - 1, n_seg)
    sp = lax.rem(si + 1, n_seg)
    sides = ((cm, si), (cp, si), (ci, sm), (ci, sp))
    barrier = pltpu.get_barrier_semaphore()
    MESH = pl.DeviceIdType.MESH
    for c in (cm, cp):
        pl.semaphore_signal(barrier, inc=1, device_id=(c, si), device_id_type=MESH)
    for k in range(1, n_seg):
        pl.semaphore_signal(
            barrier, inc=1, device_id=(ci, lax.rem(si + k, n_seg)), device_id_type=MESH
        )


    faces = 6 * e
    pair = 2 * cap
    small[1].wait()
    derivs = (d0, d1, d2)

    def codes(rows):
        k = iota((rows, faces), 1)
        return (6 * (k % e) + k // e).astype(F32)

    for r in range(4):
        k = iota((cap, 2 * e), 1)
        code = (6 * (k % e) + k // e + 2 * (r // 2)).astype(F32)
        want = column(send[0, r : r + 1, :].astype(F32), cap)
        hit = jnp.where(code == want, 1.0, 0.0).astype(BF16)
        sendpick[r * cap : (r + 1) * cap, :] = jnp.concatenate([hit, hit], axis=1)

    small[0].wait()
    density = jnp.broadcast_to(1.0 / column(mat[0:1, :], e), (e, NODES))
    lame = jnp.broadcast_to(column(mat[1:2, :], e), (e, NODES))
    shear = jnp.broadcast_to(column(mat[2:3, :], e), (e, NODES))

    loads[early[0]].wait()
    low_half = iota((e, 2 * FACE), 1) < FACE

    def comps(d):
        return [V[d][0] - 3, V[d][1] - 3, V[d][2] - 3, 6, 7, 8]

    def rows(d):
        return [0, 1, 2, V[0][d], V[1][d], V[2][d]]

    lane = iota((e, 2 * FACE), 1)
    spot = lane % FACE
    group = spot // (2 * NP)

    def paths(d):
        stride = (None, 1, NP)[d]
        start = spot % (2 * NP) // NP * FACE + spot % NP * stride
        reach = FACE - NP if d == 1 else NP - 1
        return start + jnp.where(low_half, 0, reach)

    def gather(v, path):
        return jnp.take_along_axis(v, path, axis=1, mode="promise_in_bounds")

    def trace_pair(a, b, d):
        picks = []
        path = paths(d)
        for v in (a, b):
            got = gather(v[:, : 2 * FACE], path)
            for j in range(1, 4):
                part = gather(v[:, j * 2 * FACE : (j + 1) * 2 * FACE], path)
                got = jnp.where(group == j, part, got)
            picks.append(got)
        a, b = picks
        return (
            jnp.where(low_half, a, pltpu.roll(b, FACE, 1)),
            jnp.where(low_half, pltpu.roll(a, FACE, 1), b),
        )

    def lift_paths(d):
        along = lane % FACE // NP if d == 1 else lane % NP
        across = lane % NP if d == 1 else lane % FACE // NP
        back = lane // FACE * NP + across
        gain = jnp.where(along == 0, GAIN, jnp.where(along == NP - 1, -GAIN, 0.0))
        starts = [
            jnp.where(along == NP - 1, FACE, 0) + j * 2 * NP + back for j in range(4)
        ]
        return starts, gain.astype(F32)

    def lift(v, d):
        starts, gain = lift_paths(d)
        return jnp.concatenate([gather(v, path) * gain for path in starts], axis=1)

    def face_copy(step, r):
        return pltpu.make_async_remote_copy(
            src_ref=outbox.at[step, r],
            dst_ref=inbox.at[step, r ^ 1],
            send_sem=send_sem.at[step, r],
            recv_sem=recv_sem.at[step, r ^ 1],
            device_id=sides[r],
            device_id_type=MESH,
        )

    def tie_copy(r):
        return pltpu.make_async_remote_copy(
            src_ref=tie_out.at[r - 2],
            dst_ref=tie_in.at[(r ^ 1) - 2],
            send_sem=tie_send.at[r - 2],
            recv_sem=tie_recv.at[(r ^ 1) - 2],
            device_id=sides[r],
            device_id_type=MESH,
        )

    def send_side(step, d, source):
        picked = dot(sendpick[d * pair : (d + 1) * pair, :], source)
        outbox[step, 2 * d : 2 * d + 2] = picked.reshape(2, cap, 6 * FACE)
        for r in (2 * d, 2 * d + 1):
            face_copy(step, r).start()

    def y_faces():
        trace = lame * (w[3] + w[4] + w[5])
        images = [shear * w[V[1][k]] for k in range(3)]
        images[1] = 2.0 * images[1] + trace
        images += [density * w[k] for k in range(3)]
        pairs = [trace_pair(images[2 * p], images[2 * p + 1], 1) for p in range(3)]
        return jnp.concatenate(
            [jnp.concatenate([p[s] for p in pairs], axis=1) for s in range(2)], axis=0
        )

    def x_faces():
        sides2 = []
        for s, cols in ((0, slice(0, 2 * FACE)), (1, slice(NODES - 2 * FACE, NODES))):
            rho, lam, mu = narrow
            trace = lam * (w[3, :, cols] + w[4, :, cols] + w[5, :, cols])
            images = [mu * w[V[0][k], :, cols] for k in range(3)]
            images[0] = 2.0 * images[0] + trace
            images += [rho * w[k, :, cols] for k in range(3)]
            values = []
            for p in range(3):
                a, b = images[2 * p], images[2 * p + 1]
                if s == 0:
                    values.append(jnp.where(low_half, a, pltpu.roll(b, FACE, 1)))
                else:
                    values.append(jnp.where(low_half, pltpu.roll(a, FACE, 1), b))
            sides2.append(jnp.concatenate(values, axis=1))
        return jnp.concatenate(sides2, axis=0)

    def send_y(step, both):
        send_side(step, 1, jnp.concatenate(split(both), axis=0))
        held[...] = both

    def send_x(step, both):
        high, low = split(both)
        table[: 2 * e, :] = high
        table[4 * e : 6 * e, :] = low
        send_side(step, 0, jnp.concatenate([high, low], axis=0))

    def edges(blocks, d):
        line, across = spot // NP, spot % NP
        path = jnp.where(line == NP - 1, FACE, 0) + jnp.where(low_half, 0, FACE - NP) + across
        gain = jnp.where(line == 0, GAIN, jnp.where(line == NP - 1, -GAIN, 0.0)).astype(F32)
        rho, lam, mu = (v * gain for v in narrow)
        u = [rho * gather(blocks[k], path) for k in range(3)]
        a, b = gather(blocks[3], path), gather(blocks[4], path)
        images = [lam * b, mu * a] if d == 0 else [mu * b, lam * a]
        return images + [None] + u

    def paired(images):
        sides2 = [[], []]
        for p in range(3):
            a, b = images[2 * p], images[2 * p + 1]
            if a is None:
                sides2[0].append(jnp.where(low_half, 0.0, pltpu.roll(b, FACE, 1)))
                sides2[1].append(jnp.where(low_half, 0.0, b))
            else:
                sides2[0].append(jnp.where(low_half, a, pltpu.roll(b, FACE, 1)))
                sides2[1].append(jnp.where(low_half, pltpu.roll(a, FACE, 1), b))
        return jnp.concatenate([jnp.concatenate(v, axis=1) for v in sides2], axis=0)

    def swap(v):
        n = v.shape[0]
        low = iota((n, 2 * FACE), 1) < FACE
        r = [pltpu.roll(v[:, k * 2 * FACE : (k + 1) * 2 * FACE], FACE, 1) for k in range(3)]
        return jnp.concatenate(
            [jnp.where(low, r[(k + 1) % 3], r[(k + 2) % 3]) for k in range(3)], axis=1
        )

    def onto_first(first, last):
        first, last = first * GAIN, last * -GAIN
        pieces = []
        for c in range(6):
            p, odd = c // 2, c % 2
            a = first[:, p * 2 * FACE : (p + 1) * 2 * FACE]
            b = last[:, p * 2 * FACE : (p + 1) * 2 * FACE]
            if odd:
                a = pltpu.roll(a, FACE, 1)
            else:
                b = pltpu.roll(b, FACE, 1)
            pieces.append((jnp.where(low_half, a, 0.0), jnp.where(low_half, 0.0, b)))
        return pieces

    def face_rows(lower, upper):
        blocks = []
        for c in range(6):
            p, odd = c // 2, c % 2
            a = lower[:, p * 2 * FACE : (p + 1) * 2 * FACE]
            b = upper[:, p * 2 * FACE : (p + 1) * 2 * FACE]
            if odd:
                a = pltpu.roll(a, FACE, 1)
            else:
                b = pltpu.roll(b, FACE, 1)
            blocks.append(jnp.where(low_half, a, b))
        return blocks

    narrow = [v[:, : 2 * FACE] for v in (density, lame, shear)]
    scale = jnp.concatenate(
        [
            jnp.where(low_half, narrow[2], 2.0 * narrow[2] + narrow[1]),
            jnp.where(low_half, narrow[2], narrow[0]),
            narrow[0],
        ],
        axis=1,
    )
    scale0 = jnp.concatenate(
        [
            jnp.where(low_half, 2.0 * narrow[2] + narrow[1], narrow[2]),
            jnp.where(low_half, narrow[2], narrow[0]),
            narrow[0],
        ],
        axis=1,
    )
    for k in early[1:] + (5, 4):
        loads[k].start()
    first = y_faces(), x_faces()
    pl.semaphore_wait(barrier, 1 + n_seg)
    send_y(0, first[0])
    send_x(0, first[1])
    code = codes(e)
    wants = []
    for copy in small[2:]:
        copy.wait()
    for f in range(6):
        want = column(partner[f : f + 1, :].astype(F32), e)
        wants.append(want)
        hit = jnp.where(code == want, 1.0, 0.0).astype(BF16)
        outer, inner = hit[:, : 4 * e], hit[:, 4 * e :]
        pick[f * e : (f + 1) * e, :] = jnp.concatenate([outer, outer, inner, inner], axis=1)
        if f < 4:
            slot_code = (iota((e, pair), 1) + faces + (f // 2) * pair).astype(F32)
            far = jnp.where(slot_code == want, 1.0, 0.0).astype(BF16)
            far_pick[f * e : (f + 1) * e, :] = jnp.concatenate([far, far], axis=1)
    coef0[:e, :] = GAIN * scale0
    coef0[e:, :] = -GAIN * scale0
    coef[:e, :] = GAIN * scale
    coef[e:, :] = -GAIN * scale
    ties = jnp.concatenate(
        [
            jnp.concatenate([GAIN * scale, jnp.broadcast_to(wants[2], (e, 2 * FACE))], axis=1),
            jnp.concatenate([-GAIN * scale, jnp.broadcast_to(wants[3], (e, 2 * FACE))], axis=1),
        ],
        axis=0,
    )
    picked = dot(sendpick[pair:, :], jnp.concatenate(split(ties), axis=0))
    tie_out[...] = picked.reshape(2, cap, 8 * FACE)
    for r in (2, 3):
        tie_copy(r).start()
    late[...] = jnp.zeros_like(late)
    own = si.astype(F32)
    kids = mig[...].astype(F32)
    owner, slot, octant = kids[0:1, :], kids[1:2, :], kids[2:3, :]
    key = jnp.where(owner == own, slot, parents + owner * SLOTS + slot)
    key_col = column(key, e)
    earlier = jnp.where(key_col < jnp.broadcast_to(key, (e, e)), 1.0, 0.0)
    rank = jnp.sum(earlier, axis=0, keepdims=True) * 0.125
    rank_col = column(rank, e)
    place = octant * parents + rank
    perm = jnp.where(iota((e, e), 0).astype(F32) == jnp.broadcast_to(place, (e, e)), 1.0, 0.0)
    perm = perm.astype(BF16)
    perm = jnp.concatenate([perm, perm], axis=1)
    per = 9 // GROUPS
    tiles = NODES // 128
    wide = 2 * tiles * parents
    strip = iota((e, wide), 1)
    member = rank_col == (strip % parents).astype(F32)
    group_key = jnp.sum(jnp.where(member, key_col, 0.0), axis=0, keepdims=True) * 0.125
    chunk = SLOTS * tiles
    total_rows = n_seg * chunk
    row = iota((total_rows, wide), 0)
    col = iota((total_rows, wide), 1)
    wanted = (parents + row // tiles).astype(F32)
    match = jnp.where(wanted == jnp.broadcast_to(group_key, (total_rows, wide)), 1.0, 0.0)
    same = (row % tiles) == (col // parents) % tiles
    chooser = jnp.where(same, match, 0.0).astype(BF16)
    nrow = tiles * parents
    family = child[...].astype(F32)
    holder = column(family[0:1, :], nrow)
    fslot = jnp.maximum(column(family[1:2, :], nrow), 0.0)
    at_home = holder == own
    r = iota((nrow, wide), 0)
    c = iota((nrow, wide), 1)
    home = (r % parents).astype(F32) == jnp.broadcast_to(group_key, (nrow, wide))
    home = jnp.where(home, 1.0, 0.0) * jnp.where(at_home, 1.0, 0.0)
    home = jnp.where(r // parents == (c // parents) % tiles, home, 0.0).astype(BF16)
    r = iota((nrow, total_rows), 0)
    c = iota((nrow, total_rows), 1)
    source = (holder * SLOTS + fslot) == (c // tiles).astype(F32)
    away = jnp.where(source, 1.0, 0.0) * jnp.where(at_home, 0.0, 1.0)
    away = jnp.where(r // parents == c % tiles, away, 0.0).astype(BF16)
    for g in range(GROUPS):
        arrived[g, pl.ds(si, 1)] = jnp.zeros((1, chunk, per * 128), F32)
    for k in early[1:]:
        loads[k].wait()

    def three(picks, cols=slice(0, NODES)):
        high = jnp.concatenate([xh[c * e : (c + 1) * e, cols] for c in picks], axis=0)
        low = jnp.concatenate([xl[c * e : (c + 1) * e, cols] for c in picks], axis=0)
        return jnp.concatenate([high, low, high], axis=1)

    def stage(step, carry):
        trace = lame * (w[3] + w[4] + w[5])
        fields = [2.0 * (shear * w[3 + k]) + trace for k in range(3)]
        fields += [shear * w[6 + k] for k in range(3)]
        fields += [density * w[k] for k in range(3)]
        high, low = split(held[...])
        table[2 * e : 4 * e, :] = high
        table[6 * e : 8 * e, :] = low
        near = dot(pick[:, : 8 * e], table[: 8 * e, :])
        for k in range(9):
            high, low = split(fields[k])
            xh[k * e : (k + 1) * e, :] = high
            xl[k * e : (k + 1) * e, :] = low

        part0 = dot(three(comps(0)), d0[...])
        keep = jnp.where(step == 0, -4.0 / 3.0, jnp.where(step == 2, 2.0 / 3.0, 1.0 / 3.0))
        keep = keep.astype(F32)
        for k in range(9):
            out[k] = jnp.where(step == 0, 0.0, out[k]) + keep * w[k]

        cd = comps(2)
        for p in range(3):
            cols = slice(p * 2 * FACE, (p + 1) * 2 * FACE)
            pair2 = trace_pair(fields[cd[2 * p]], fields[cd[2 * p + 1]], 2)
            for s, value in enumerate(pair2):
                high, low = split(value)
                table[(8 + s) * e : (9 + s) * e, cols] = high
                table[(10 + s) * e : (11 + s) * e, cols] = low
        near = near + dot(pick[:, 8 * e :], table[8 * e :, :])
        side = [near[f * e : (f + 1) * e, :] for f in range(6)]
        ahead = jnp.where(step < 2, 0.5 * STEP, jnp.where(step == 2, STEP, STEP / 6.0))
        ahead = ahead.astype(F32)
        seen = set()
        for d in range(3):
            if d == 0:
                parts = [part0]
            else:
                sides2 = face_rows(side[2 * d], side[2 * d + 1])
                if d == 1:
                    lifts = [lift(v, d) for v in sides2]
                    parts = [
                        dot(three(comps(d), slice(h * HALF, (h + 1) * HALF)), derivs[d][...])
                        for h in range(2)
                    ]
                else:
                    edge = jnp.concatenate(split(jnp.concatenate(sides2, axis=0)), axis=1)
                    parts = [
                        dot(
                            jnp.concatenate(
                                [three(comps(d), slice(h * HALF, (h + 1) * HALF)), edge], axis=1
                            ),
                            jnp.concatenate(
                                [derivs[d][...], spread[:, h * HALF : (h + 1) * HALF]], axis=0
                            ),
                        )
                        for h in range(2)
                    ]
            width = NODES // len(parts)
            for c, row in enumerate(rows(d)):
                for h, part in enumerate(parts):
                    piece = part[c * e : (c + 1) * e, :]
                    cols = slice(h * width, (h + 1) * width)
                    if d == 1:
                        piece = piece + lifts[c][:, cols]
                    if row in seen:
                        vol[row, :, cols] += piece
                    else:
                        vol[row, :, cols] = piece
                seen.add(row)
        for row, (a, b) in zip(rows(0), onto_first(side[0], side[1])):
            vol[row, :, : 2 * FACE] += a
            vol[row, :, -2 * FACE :] += b
        for k in range(9):
            w[k] = adj[k] + ahead * vol[k]

        def far(d, got):
            high, low = split(got)
            far_table[d, :pair, :] = high
            far_table[d, pair:, :] = low
            return dot(far_pick[2 * d * e : 2 * (d + 1) * e, :], far_table[d])

        def arrive(d):
            for r in (2 * d, 2 * d + 1):
                face_copy(step, r).wait()
            got = inbox[step, 2 * d : 2 * d + 2].reshape(pair, 6 * FACE)
            if d == 1:
                got = got + late[...]
            picked = far(d, got)
            return picked, face_rows(picked[:e], picked[e:])

        def apply_x(picked):
            for row, (a, b) in zip(rows(0), onto_first(picked[:e], picked[e:])):
                w[row, :, : 2 * FACE] += ahead * a
                w[row, :, -2 * FACE :] += ahead * b

        def apply_y(blocks):
            edge = jnp.concatenate(split(jnp.concatenate(blocks, axis=0)), axis=1)
            lifted = dot(edge, spread_y[...])
            for c, row in enumerate(rows(1)):
                w[row] += ahead * lifted[c * e : (c + 1) * e, :]

        base = y_faces()
        base_x = x_faces()

        @pl.when(step < 3)
        def _():
            picked, blocks = arrive(0)
            send_y(step + 1, base + ahead * paired(edges(blocks, 1)))
            ready_x = base_x + ahead * (coef0[...] * swap(picked))
            apply_x(picked)
            picked, blocks = arrive(1)
            source = jnp.concatenate(
                [table[2 * e : 4 * e, :], table[6 * e : 8 * e, :]], axis=0
            )
            send_x(step + 1, ready_x + ahead * paired(edges(blocks, 0)))
            apply_y(blocks)
            held[...] = held[...] + ahead * (coef[...] * swap(picked))

            @pl.when(step == 0)
            def _():
                for r in (2, 3):
                    tie_copy(r).wait()
                told = tie_in[:, :, 6 * FACE :].reshape(pair, 2 * FACE)[:, :pair]
                slot = iota((pair, pair), 1)
                mine = faces + (3 - slot // cap) * cap + slot % cap
                link = jnp.where(told == mine.astype(F32), 1.0, 0.0).astype(BF16)
                echo[...] = dot(link, sendpick[pair:, :]).astype(BF16)

            ours = dot(echo[...], source)
            late[...] = ahead * (tie_in[:, :, : 6 * FACE].reshape(pair, 6 * FACE) * swap(ours))

        @pl.when(step == 3)
        def _():
            apply_x(arrive(0)[0])
            apply_y(arrive(1)[1])

        return carry

    lax.fori_loop(0, 4, stage, 0)
    for k in (4, 5):
        loads[k].wait()

    def fold(values, matrix, ways, blocks):
        count = len(values)
        groups = [[] for _ in range(ways)]
        for v in values:
            octants = v.shape[0] // parents
            for way in range(ways):
                for c in range(way, octants, ways):
                    groups[way].append(v[c * parents : (c + 1) * parents, :])
        sides2 = [split(jnp.concatenate(p, axis=0)) for p in groups]
        width = NODES // blocks
        results = []
        for h in range(blocks):
            cols = slice(h * width, (h + 1) * width)
            high = jnp.concatenate([s[0][:, cols] for s in sides2], axis=1)
            low = jnp.concatenate([s[1][:, cols] for s in sides2], axis=1)
            results.append(dot(jnp.concatenate([high, low, high], axis=1), matrix[...]))
        total = results[0] if blocks == 1 else jnp.concatenate(results, axis=1)
        m = total.shape[0] // count
        return [total[k * m : (k + 1) * m, :] for k in range(count)]

    def migration_copy(g, k):
        to = lax.rem(si + k, n_seg)
        return pltpu.make_async_remote_copy(
            src_ref=pay.at[g, to],
            dst_ref=arrived.at[g, si],
            send_sem=mig_send.at[g, k - 1],
            recv_sem=mig_recv.at[g, k - 1],
            device_id=(ci, to),
            device_id_type=MESH,
        )

    local = []
    for g in range(GROUPS):
        ordered = []
        for k in range(g * per, (g + 1) * per):
            total = out[k] + w[k]
            out[k] = total
            ordered.append(dot(perm, jnp.concatenate(split(total), axis=0)))
        sums = fold(fold(ordered, r1, 4, 2), r0, 2, 1)
        stacked = jnp.concatenate(
            [
                jnp.concatenate([s[:, k * 128 : (k + 1) * 128] for s in sums], axis=1)
                for k in range(tiles)
            ],
            axis=0,
        )
        both = jnp.concatenate(split(stacked), axis=0)
        pay[g] = dot(chooser, both).reshape(n_seg, chunk, per * 128)
        for k in range(1, n_seg):
            migration_copy(g, k).start()
        local.append(dot(home, both))
    for g in range(GROUPS):
        for k in range(1, n_seg):
            migration_copy(g, k).wait()
        ah, al = split(arrived[g].reshape(total_rows, per * 128))
        result = local[g] + dot(
            jnp.concatenate([away, away], axis=1), jnp.concatenate([ah, al], axis=0)
        )
        for k in range(per):
            for t in range(tiles):
                par[g * per + k, :, t * 128 : (t + 1) * 128] = result[
                    t * parents : (t + 1) * parents, k * 128 : (k + 1) * 128
                ]


def hand_over(a_in, b_in, a_out, b_out, sems):
    copies = [
        pltpu.make_async_copy(a_in, a_out, sems.at[0]),
        pltpu.make_async_copy(b_in, b_out, sems.at[1]),
    ]
    for copy in copies:
        copy.start()
    for copy in copies:
        copy.wait()


def shards(n_curve, n_seg, adjoint, material, face_partner, send_faces, migration, children):
    e = adjoint.shape[1]
    cap = send_faces.shape[2]
    parents = children.shape[1]
    tables = [jnp.asarray(m) for m in constants()]
    faces, pair = 6 * e, 2 * cap
    chunk = SLOTS * (NODES // 128)
    vmem = pl.BlockSpec(memory_space=pltpu.VMEM)
    away = pl.BlockSpec(memory_space=pl.ANY)
    dma = pltpu.SemaphoreType.DMA
    shapes = (
        jax.ShapeDtypeStruct((9, e, NODES), F32),
        jax.ShapeDtypeStruct((9, parents, NODES), F32),
    )
    results = pl.pallas_call(
        functools.partial(kernel, n_curve, n_seg, e, cap, parents),
        out_shape=tuple(pltpu.VMEM(x.shape, F32) for x in shapes),
        in_specs=[away] * (6 + len(tables)),
        out_specs=(vmem, vmem),
        scratch_shapes=[
            pltpu.VMEM((3, e), F32),
            pltpu.VMEM((6, e), jnp.int32),
            pltpu.VMEM(send_faces.shape, jnp.int32),
            pltpu.VMEM((3, e), jnp.int32),
            pltpu.VMEM((2, parents), jnp.int32),
            pltpu.VMEM((9, e, NODES), F32),
        ]
        + [pltpu.VMEM(m.shape, BF16) for m in tables]
        + [
            pltpu.VMEM((9, e, NODES), F32),
            pltpu.VMEM((9 * e, NODES), BF16),
            pltpu.VMEM((9 * e, NODES), BF16),
            pltpu.VMEM((9, e, NODES), F32),
            pltpu.VMEM((2 * faces, 6 * FACE), BF16),
            pltpu.VMEM((2, 2 * pair, 6 * FACE), BF16),
            pltpu.VMEM((faces, 2 * faces), BF16),
            pltpu.VMEM((4 * e, 2 * pair), BF16),
            pltpu.VMEM((2 * pair, 4 * e), BF16),
            pltpu.VMEM((4, 4, cap, 6 * FACE), F32),
            pltpu.VMEM((4, 4, cap, 6 * FACE), F32),
            pltpu.VMEM((2, cap, 8 * FACE), F32),
            pltpu.VMEM((2, cap, 8 * FACE), F32),
            pltpu.VMEM((2 * e, 6 * FACE), F32),
            pltpu.VMEM((2 * e, 6 * FACE), F32),
            pltpu.VMEM((2 * e, 6 * FACE), F32),
            pltpu.VMEM((pair, 6 * FACE), F32),
            pltpu.VMEM((pair, 4 * e), BF16),
            pltpu.VMEM((GROUPS, n_seg, chunk, 9 // GROUPS * 128), F32),
            pltpu.VMEM((GROUPS, n_seg, chunk, 9 // GROUPS * 128), F32),
            dma((5,)),
            dma((9,)),
            dma((4, 4)),
            dma((4, 4)),
            dma((2,)),
            dma((2,)),
            dma((GROUPS, n_seg - 1)),
            dma((GROUPS, n_seg - 1)),
        ],
        compiler_params=pltpu.CompilerParams(
            collective_id=0, has_side_effects=True, vmem_limit_bytes=60 * 2**20
        ),
    )(material, send_faces, face_partner.T, migration, children, adjoint, *tables)
    return pl.pallas_call(
        hand_over,
        out_shape=shapes,
        in_specs=[vmem, vmem],
        out_specs=(away, away),
        scratch_shapes=[dma((2,))],
    )(*(pltpu.with_memory_space_constraint(x, pltpu.VMEM) for x in results))


def solution(mesh):
    both = ("curve", "seg")
    in_specs = (
        P(None, both, None),
        P(None, both),
        P(both, None),
        P(both, None, None),
        P(None, both),
        P(None, both),
    )
    out_specs = (P(None, both, None), P(None, both, None))
    body = functools.partial(shards, mesh.shape["curve"], mesh.shape["seg"])
    return jax.shard_map(
        body, mesh=mesh, in_specs=in_specs, out_specs=out_specs, check_vma=False
    )
```
